32 devices in a mesh: groups: 2 (over y), offset: 4 (over x, core), space: 4 (over z).
Axes of the slice: x: 2, y: 2, z: 4, core: 2. Of those that a mesh axis runs over, the one named last changes fastest.
Arguments:
- src_now: float32 [4, 256, 2048], P('offset', ('groups', 'space')), parts along dimension 1, may hold values from -6 to 6
- src_prev: float32 [4, 256, 2048], P('offset', ('groups', 'space')), parts along dimension 1, may hold values from -6 to 6
- rcv_now: float32 [4, 256, 2048], P('offset', ('groups', 'space')), parts along dimension 1, may hold values from -6 to 6
- rcv_prev: float32 [4, 256, 2048], P('offset', ('groups', 'space')), parts along dimension 1, may hold values from -6 to 6
- courant: float32 [256, 2048], P(('groups', 'space')), parts along dimension 0, may hold values from 0.05 to 0.2
- shot_cell: int32 [8], P('groups'), parts along dimension 0, may hold values from 0 to 262143
- wavelet: float32 [8], P('groups'), parts along dimension 0, may hold values from 4 to 8
- shifts: int32 [128], replicated, may hold values from -64 to 64
- angle_map: float32 [128, 128], replicated, may hold values from -0.5 to 0.5
Outputs:
- angle_image: float32 [128, 256, 2048], P(None, ('groups', 'space'), 'offset'), parts along dimension 1
The draws below stay inside these ranges and needn't reach their ends.
There are 2 independent parts, one for each index of `groups`. The reference program is written for one: setup_inputs(seed, part) draws one part's arguments, and reference() takes and returns one part's arrays. A program takes and returns all parts, laid end to end along the dimension named above; an argument that names none is the same for every part. Nothing has to cross between parts.
All inputs are finite; a program needn't handle non-finite values.
Results may differ from the reference program's by a relative error of at most 0.0003.
Values sent between devices are 32-bit elements; how exact they have to be, the bound alone decides.
No kernel may reach another device: no remote copies, remote signals or barrier semaphores. Data moves between devices by JAX's collectives and lax.ppermute only.
A program may use at most 128 MiB of HBM per device.

```python
import jax
import jax.numpy as jnp
from jax import lax

NX = 2048
H = 128
A = 128
MAXLAG = 64
NSHOT = 4
NZ = 128


def with_ends(values, key, smallest, high):
    spot = [jax.random.randint(jax.random.fold_in(key, axis), (), 0, length) for axis, length in enumerate(values.shape)]
    main_axis = values.shape.index(max(values.shape))
    beside = spot[:main_axis] + [(spot[main_axis] + 1) % values.shape[main_axis]] + spot[main_axis + 1:]
    return values.at[tuple(spot)].set(smallest).at[tuple(beside)].set(high)


def levels(key, extent, cuts, low, largest):
    def one(dim, parts):
        steps = jax.random.uniform(jax.random.fold_in(jax.random.fold_in(key, 6), dim), (parts,), jnp.float32, low / len(cuts), largest / len(cuts))
        return jnp.repeat(jnp.exp(steps), extent[dim] // parts).reshape((-1,) + (1,) * (len(extent) - dim - 1))

    factor_of = one(*cuts[0])
    for cut in cuts[1:]:
        factor_of = factor_of * one(*cut)
    return factor_of


def normal_values(own_key, extent, width, most, cuts=(), kind=jnp.bfloat16):
    values = jax.random.normal(own_key, extent, jnp.float32) * width
    if len(cuts) > 0:
        values = levels(own_key, extent, cuts, -0.22, 0.18) * values
    return jnp.clip(values, min=-most, max=most).astype(kind)


def setup_inputs(seed: int = 0, part: int = 0) -> dict:
    key_list = jax.random.split(jax.random.key(seed), 10)
    part_keys = jax.random.split(jax.random.fold_in(key_list[9], part), 10)
    return {
        "src_now": normal_values(part_keys[0], (NSHOT, NZ, NX), 1.0, 6.0, ((0, 4), (1, 4)), jnp.float32),
        "src_prev": normal_values(part_keys[1], (NSHOT, NZ, NX), 1.0, 6.0, ((0, 4), (1, 4)), jnp.float32),
        "rcv_now": normal_values(part_keys[2], (NSHOT, NZ, NX), 1.0, 6.0, ((0, 4), (1, 4)), jnp.float32),
        "rcv_prev": normal_values(part_keys[3], (NSHOT, NZ, NX), 1.0, 6.0, ((0, 4), (1, 4)), jnp.float32),
        "courant": jnp.clip(0.05 + 0.15 * jax.random.uniform(part_keys[4], (NZ, NX), jnp.float32) ** levels(part_keys[4], (NZ, NX), ((0, 4),), -0.2, 0.2), 0.05, 0.2),
        "shot_cell": with_ends(jax.random.randint(part_keys[5], (NSHOT,), 0, NZ * NX), jax.random.fold_in(part_keys[5], 1), 0, (NZ * NX) - 1).astype(jnp.int32),
        "wavelet": jnp.clip(jax.random.uniform(part_keys[6], (NSHOT,), jnp.float32, 4.0, 8.0), 4.0, 8.0),
        "shifts": with_ends(jax.random.randint(key_list[7], (H,), 0 - MAXLAG, MAXLAG + 1), jax.random.fold_in(key_list[7], 1), 0 - MAXLAG, MAXLAG).astype(jnp.int32),
        "angle_map": normal_values(key_list[8], (A, H), H ** -0.5, 0.5, (), jnp.float32),
    }


coeffs = (-205.0 / 72.0, 8.0 / 5.0, -1.0 / 5.0, 8.0 / 315.0, -1.0 / 560.0)


def laplace(field):
    nz = field.shape[-2]
    nx = field.shape[-1]
    padded = jnp.pad(field, ((0, 0), (4, 4), (4, 4)))
    total = 2.0 * coeffs[0] * field
    for k in range(1, 5):
        total = total + coeffs[k] * (padded[:, 4 - k:4 - k + nz, 4:4 + nx] + padded[:, 4 + k:4 + k + nz, 4:4 + nx] + padded[:, 4:4 + nz, 4 - k:4 - k + nx] + padded[:, 4:4 + nz, 4 + k:4 + k + nx])
    return total


def reference(src_now, src_prev, rcv_now, rcv_prev, courant, shot_cell, wavelet, shifts, angle_map):
    nz = src_now.shape[1]
    nx = src_now.shape[2]
    src_next = 2.0 * src_now - src_prev + courant[None] * laplace(src_now)
    flat = (lax.broadcasted_iota(jnp.int32, (nz, nx), 0) * nx + lax.broadcasted_iota(jnp.int32, (nz, nx), 1))
    onehot = (flat[None] == shot_cell[:, None, None]).astype(jnp.float32)
    src_next = src_next + wavelet[:, None, None] * onehot
    rcv_next = 2.0 * rcv_now - rcv_prev + courant[None] * laplace(rcv_now)
    src_pad = jnp.pad(src_next, ((0, 0), (0, 0), (MAXLAG, MAXLAG)))
    rcv_pad = jnp.pad(rcv_next, ((0, 0), (0, 0), (MAXLAG, MAXLAG)))

    def one_offset(lag):
        left = lax.dynamic_slice_in_dim(src_pad, (MAXLAG - lag).astype(jnp.int32), nx, 2)
        right = lax.dynamic_slice_in_dim(rcv_pad, (MAXLAG + lag).astype(jnp.int32), nx, 2)
        return jnp.sum(left * right, 0)

    image = lax.map(one_offset, shifts)
    return jnp.einsum("ah,hzx->azx", angle_map, image, precision=lax.Precision.HIGHEST)
```

```python
import functools

import jax
import jax.numpy as jnp
from jax import lax
from jax.experimental import pallas as pl
from jax.experimental.pallas import tpu as pltpu
from jax.sharding import PartitionSpec as P

MAXLAG = 64
LANES = 128
ROWS = 2 * LANES
GROUP = 8
RIM = 4
PITCH = LANES + 1
MB = 4
NB = 4
MARGIN = 8

coeffs = (-205.0 / 72.0, 8.0 / 5.0, -1.0 / 5.0, 8.0 / 315.0, -1.0 / 560.0)


def split(x):
    high = x.astype(jnp.bfloat16)
    low = (x - high.astype(jnp.float32)).astype(jnp.bfloat16)
    return high, low


def edge_body(src_top, src_low, rcv_top, rcv_low, up_ref, down_ref):
    up_ref[0:RIM, :] = src_top[0, 0:RIM, :]
    up_ref[RIM : 2 * RIM, :] = rcv_top[0, 0:RIM, :]
    down_ref[0:RIM, :] = src_low[0, GROUP - RIM : GROUP, :]
    down_ref[RIM : 2 * RIM, :] = rcv_low[0, GROUP - RIM : GROUP, :]


def edge_rows(src_now, rcv_now):
    depth, nx = src_now.shape[1:]
    top = pl.BlockSpec((1, GROUP, nx), lambda i: (0, 0, 0))
    low = pl.BlockSpec((1, GROUP, nx), lambda i: (0, depth // GROUP - 1, 0))
    return pl.pallas_call(
        edge_body,
        grid=(1,),
        in_specs=[top, low, top, low],
        out_specs=[pl.BlockSpec((GROUP, nx), lambda i: (0, 0))] * 2,
        out_shape=[jax.ShapeDtypeStruct((GROUP, nx), jnp.float32)] * 2,
        name="edge_rows",
    )(src_now, src_now, rcv_now, rcv_now)


def stepped(ext, prev, courant, rows):
    nx = ext.shape[1]
    cols = lax.broadcasted_iota(jnp.int32, (rows, nx), 1)
    now = ext[RIM : RIM + rows, :]
    total = (2.0 * coeffs[0]) * now
    for k in range(1, RIM + 1):
        left = jnp.where(cols < k, 0.0, pltpu.roll(now, k, 1))
        right = jnp.where(cols >= nx - k, 0.0, pltpu.roll(now, nx - k, 1))
        total = total + coeffs[k] * (ext[RIM - k : RIM - k + rows, :] + ext[RIM + k : RIM + k + rows, :] + left + right)
    return 2.0 * now - prev + courant * total


def injected(value, first_row, nx, cell, amp):
    rows = lax.broadcasted_iota(jnp.int32, value.shape, 0) + first_row
    flat = rows * nx + lax.broadcasted_iota(jnp.int32, value.shape, 1)
    return value + jnp.where(flat == cell, amp, 0.0)


def spread(padded, outs, width):
    me = lax.axis_index("offset")
    for d, out in enumerate(outs):
        first = pl.multiple_of(lax.bitwise_xor(me, d) * width, LANES)
        out[...] = padded[:, :, pl.ds(first, width + 2 * MAXLAG)]


def place(padded, f, row, value):
    rows, nx = value.shape
    zero = jnp.zeros((rows, MAXLAG), jnp.float32)
    padded[f, row : row + rows, :] = jnp.concatenate([zero, value, zero], 1)


def inner_body(width, cell_ref, amp_ref, src_now, src_prev, rcv_now, rcv_prev, courant, *refs):
    outs, padded = refs[:-1], refs[-1]
    depth, nx = src_now.shape[1:]
    me = lax.axis_index("offset")
    slab = lax.axis_index("space") * depth
    for f, (now, prev) in enumerate(((src_now, src_prev), (rcv_now, rcv_prev))):
        for z in range(GROUP, depth - GROUP, GROUP):
            value = stepped(now[0, z - RIM : z + GROUP + RIM, :], prev[0, z : z + GROUP, :], courant[z : z + GROUP, :], GROUP)
            if f == 0:
                value = injected(value, slab + z, nx, cell_ref[me], amp_ref[me])
            place(padded, f, z - GROUP, value)
    spread(padded, outs, width)


def outer_body(width, cell_ref, amp_ref, above, below, src_now, src_prev, rcv_now, rcv_prev, courant, *refs):
    outs, padded = refs[:-1], refs[-1]
    depth, nx = src_now.shape[1:]
    me = lax.axis_index("offset")
    slab = lax.axis_index("space") * depth
    for f, (now, prev) in enumerate(((src_now, src_prev), (rcv_now, rcv_prev))):
        for b, z in enumerate((0, depth - GROUP)):
            if b == 0:
                ext = jnp.concatenate([above[f * RIM : (f + 1) * RIM, :], now[0, 0 : GROUP + RIM, :]], 0)
            else:
                ext = jnp.concatenate([now[0, depth - GROUP - RIM : depth, :], below[f * RIM : (f + 1) * RIM, :]], 0)
            value = stepped(ext, prev[0, z : z + GROUP, :], courant[z : z + GROUP, :], GROUP)
            if f == 0:
                value = injected(value, slab + z, nx, cell_ref[me], amp_ref[me])
            place(padded, f, b * GROUP, value)
    spread(padded, outs, width)


def windows(body, name, count, rows, halos, cell, amp, fields):
    nx = fields[0].shape[2]
    width = nx // count
    out = jax.ShapeDtypeStruct((2, rows, width + 2 * MAXLAG), jnp.float32)
    smem = pl.BlockSpec(memory_space=pltpu.SMEM)
    vmem = pl.BlockSpec(memory_space=pltpu.VMEM)
    return pl.pallas_call(
        functools.partial(body, width),
        in_specs=[smem, smem] + [vmem] * (len(halos) + len(fields)),
        out_specs=[vmem] * count,
        out_shape=[out] * count,
        scratch_shapes=[pltpu.VMEM((2, rows, nx + 2 * MAXLAG), jnp.float32)],
        name=name,
    )(cell, amp, *halos, *fields)


def weight_body(shift_ref, map_ref, mw_ref, slot_ref):
    lag = lax.broadcasted_iota(jnp.int32, (ROWS, LANES), 0) - MAXLAG
    hot = jnp.where(lag == shift_ref[...], 1.0, 0.0)
    full = lax.dot_general(
        map_ref[...], hot, (((1,), (1,)), ((), ())), precision=lax.Precision.HIGHEST, preferred_element_type=jnp.float32
    )
    na = full.shape[0]
    used = jnp.max(hot[:LANES, :], axis=1, keepdims=True)
    k = lax.broadcasted_iota(jnp.int32, (LANES, 1), 0).astype(jnp.float32)
    slot = jnp.min(jnp.where(used > 0.0, float(ROWS), k), axis=0, keepdims=True).astype(jnp.int32)
    column = lax.broadcasted_iota(jnp.int32, (na, LANES), 1)
    w = jnp.where(column == slot, full[:, LANES : LANES + 1], full[:, :LANES])
    high, low = split(w)
    mw_ref[0, :, :LANES] = high
    mw_ref[0, :, LANES:] = high
    mw_ref[1, :, :LANES] = low
    mw_ref[1, :, LANES:] = jnp.zeros_like(low)
    slot_ref[...] = jnp.broadcast_to(slot, slot_ref.shape)


def angle_weights(shifts, angle_map):
    na = angle_map.shape[0]
    return pl.pallas_call(
        weight_body,
        out_shape=[jax.ShapeDtypeStruct((2, na, ROWS), jnp.bfloat16), jax.ShapeDtypeStruct((GROUP, LANES), jnp.int32)],
        name="angle_weights",
    )(shifts.reshape(1, -1), angle_map)


def products(na, shots, slot_ref, mw_ref, fwd, rev, obuf, rhs):
    slot = slot_ref[...]
    sub = lax.broadcasted_iota(jnp.int32, (GROUP, LANES), 0)
    steps = 16 // MB

    def fill(rho, mb, buf):
        extra = []
        for m in range(mb * MB, (mb + 1) * MB):
            tot = None
            for s in range(shots):
                t = rev[s, pl.ds(ROWS - 1 - 8 * m - rho, 1), :] * fwd[s, pl.ds(LANES + 8 * m + rho, 1), :]
                tot = t if tot is None else tot + t
            extra.append(jnp.broadcast_to(tot, (GROUP, LANES)))
        for nb in range(16 // NB):
            acc = [[None] * NB for _ in range(MB)]
            for s in range(shots):
                a = {}
                c = {}
                for i in range(MB):
                    for j in range(NB):
                        m, n = mb * MB + i, nb * NB + j
                        if n - m not in a:
                            a[n - m] = rev[s, pl.ds(LANES - 1 - rho + 8 * (n - m), GROUP), :]
                        if n + m not in c:
                            c[n + m] = fwd[s, pl.ds(rho + 8 * (n + m), GROUP), :]
                        t = a[n - m] * c[n + m]
                        acc[i][j] = t if acc[i][j] is None else acc[i][j] + t
            for j in range(0, NB, 2):
                n = nb * NB + j
                masks = [sub == slot - 8 * (n + k) for k in range(2)]
                for i in range(MB):
                    high, low = split(jnp.concatenate([jnp.where(masks[k], extra[i], acc[i][j + k]) for k in range(2)], 0))
                    rhs[buf, 8 * n : 8 * n + 16, i * LANES : (i + 1) * LANES] = high
                    rhs[buf, LANES + 8 * n : LANES + 8 * n + 16, i * LANES : (i + 1) * LANES] = low

    def contract(rho, mb, buf):
        res = jnp.dot(mw_ref[0], rhs[buf], preferred_element_type=jnp.float32)
        res += jnp.dot(mw_ref[1], rhs[buf], preferred_element_type=jnp.float32)
        for i in range(MB):
            obuf[pl.ds(MARGIN + 8 * (mb * MB + i) + rho, na, stride=PITCH), :] = res[:, i * LANES : (i + 1) * LANES]

    @pl.loop(0, 8)
    def _(rho):
        contract(rho - 1, steps - 1, (steps - 1) % 2)
        for mb in range(steps):
            fill(rho, mb, mb % 2)
            if mb:
                contract(rho, mb - 1, (mb - 1) % 2)

    contract(7, steps - 1, (steps - 1) % 2)


def image_body(blocks, ablk, shots, slot_ref, mw_ref, *refs):
    inner, outer = refs[:shots], refs[shots : 2 * shots]
    out_ref, fwd, rev, obuf = refs[2 * shots :]
    depth = out_ref.shape[1]

    @pl.when(pl.program_id(0) == 0)
    def _():
        rows = lax.broadcasted_iota(jnp.int32, (LANES, LANES), 0)
        cols = lax.broadcasted_iota(jnp.int32, (LANES, LANES), 1)
        anti = (rows + cols == LANES - 1).astype(jnp.float32)

        def gathered(s, f, b):
            tiles = []
            for q in range(blocks):
                at = slice((q + b) * LANES, (q + b + 1) * LANES)
                tiles += [outer[s][f, :GROUP, at], inner[s][f, :, at], outer[s][f, GROUP:, at]]
            if blocks * depth < LANES:
                tiles.append(jnp.zeros((LANES - blocks * depth, LANES), jnp.float32))
            return jnp.concatenate(tiles, 0)

        for s in range(shots):
            for b in range(2):
                fwd[s, b * LANES : (b + 1) * LANES, :] = gathered(s, 1, b).T
                rev[s, (1 - b) * LANES : (2 - b) * LANES, :] = lax.dot_general(
                    anti, gathered(s, 0, b), (((1,), (1,)), ((), ())),
                    precision=lax.Precision.HIGHEST, preferred_element_type=jnp.float32)

        pl.run_scoped(
            functools.partial(products, mw_ref.shape[1], shots, slot_ref, mw_ref, fwd, rev, obuf),
            pltpu.VMEM((2, ROWS, LANES * MB), jnp.bfloat16),
        )

    first = pl.program_id(0) * ablk
    for a in range(ablk):
        tile = obuf[pl.ds(MARGIN + (first + a) * PITCH, LANES), :].T
        for q in range(blocks):
            out_ref[a, :, q * LANES : (q + 1) * LANES] = tile[q * depth : (q + 1) * depth, :]


def angle_image(inner, outer, mw, slot, depth):
    shots = len(inner)
    full = inner[0].shape[2]
    width = full - 2 * MAXLAG
    na = mw.shape[1]
    ablk = 16
    whole = lambda x: pl.BlockSpec(x.shape, lambda i: (0,) * x.ndim)
    return pl.pallas_call(
        functools.partial(image_body, width // LANES, ablk, shots),
        out_shape=jax.ShapeDtypeStruct((na, depth, width), jnp.float32),
        grid=(na // ablk,),
        in_specs=[whole(slot), whole(mw)] + [whole(x) for x in inner + outer],
        out_specs=pl.BlockSpec((ablk, depth, width), lambda i: (i, 0, 0)),
        scratch_shapes=[
            pltpu.VMEM((shots, ROWS, LANES), jnp.float32),
            pltpu.VMEM((shots, ROWS, LANES), jnp.float32),
            pltpu.VMEM((2 * MARGIN + na * PITCH, LANES), jnp.float32),
        ],
        compiler_params=pltpu.CompilerParams(vmem_limit_bytes=56 << 20),
        name="angle_image",
    )(slot, mw, *inner, *outer)


def body(src_now, src_prev, rcv_now, rcv_prev, courant, shot_cell, wavelet, shifts, angle_map):
    depth = src_now.shape[1]
    count = lax.axis_size("offset")
    slabs = lax.axis_size("space")
    fields = (src_now, src_prev, rcv_now, rcv_prev, courant)
    up, down = edge_rows(src_now, rcv_now)
    below = lax.ppermute(up, "space", [(i + 1, i) for i in range(slabs - 1)])
    above = lax.ppermute(down, "space", [(i, i + 1) for i in range(slabs - 1)])

    def exchanged(wins):
        return [wins[0]] + [lax.ppermute(wins[d], "offset", [(i, i ^ d) for i in range(count)]) for d in range(1, count)]

    inner = exchanged(windows(inner_body, "inner_rows", count, depth - 2 * GROUP, (), shot_cell, wavelet, fields))
    outer = exchanged(windows(outer_body, "outer_rows", count, 2 * GROUP, (above, below), shot_cell, wavelet, fields))
    mw, slot = angle_weights(shifts, angle_map)
    return angle_image(inner, outer, mw, slot, depth)


def solution(mesh):
    placed = (
        P("offset", ("groups", "space"), None),
        P("offset", ("groups", "space"), None),
        P("offset", ("groups", "space"), None),
        P("offset", ("groups", "space"), None),
        P(("groups", "space"), None),
        P("groups"),
        P("groups"),
        P(),
        P(),
    )
    step = jax.shard_map(
        body,
        mesh=mesh,
        in_specs=placed,
        out_specs=P(None, ("groups", "space"), "offset"),
        check_vma=False,
    )

    def run(*args):
        with jax.sharding.use_abstract_mesh(mesh.abstract_mesh):
            return step(*args)

    return run
```

```python
import functools

import jax
import jax.numpy as jnp
from jax import lax
from jax.experimental import pallas as pl
from jax.experimental.pallas import tpu as pltpu
from jax.sharding import PartitionSpec as P

MAXLAG = 64
LANES = 128
ROWS = 2 * LANES
GROUP = 8
RIM = 4
PITCH = LANES + 1
MB = 4
NB = 4
APART = 16

coeffs = (-205.0 / 72.0, 8.0 / 5.0, -1.0 / 5.0, 8.0 / 315.0, -1.0 / 560.0)


def split(x):
    high = x.astype(jnp.bfloat16)
    low = (x - high.astype(jnp.float32)).astype(jnp.bfloat16)
    return high, low


def lateral(tiles, lane):
    zero = jnp.zeros_like(tiles[0])
    total = [None] * len(tiles)
    for k in range(1, RIM + 1):
        up = [pltpu.roll(v, k, 1) for v in tiles]
        down = [pltpu.roll(v, LANES - k, 1) for v in tiles]
        for t in range(len(tiles)):
            left = jnp.where(lane < k, up[t - 1] if t else zero, up[t])
            right = jnp.where(lane >= LANES - k, down[t + 1] if t + 1 < len(tiles) else zero, down[t])
            term = coeffs[k] * (left + right)
            total[t] = term if total[t] is None else total[t] + term
    return total


def step_rows(jobs, width, cell_ref, amp_ref, prevs, courant, rows_ref, padded, outs):
    pitch = rows_ref.shape[2]
    count = len(outs)
    nx = courant.shape[1]
    depth = courant.shape[0]
    blocks = nx // LANES
    me = lax.axis_index("offset")
    cell = cell_ref[me] - lax.axis_index("space") * depth * nx
    amp = amp_ref[me]
    lane = lax.broadcasted_iota(jnp.int32, (GROUP, LANES), 1)
    flat = lax.broadcasted_iota(jnp.int32, (GROUP, LANES), 0) * nx + lane
    source = lax.broadcasted_iota(jnp.int32, (LANES, LANES), 0)
    target = lax.broadcasted_iota(jnp.int32, (LANES, LANES), 1)
    mirror = (lax.rem(source + target + 1, LANES) == MAXLAG).astype(jnp.float32)
    half = lane < MAXLAG
    zero = jnp.zeros((GROUP, LANES), jnp.float32)
    for f in range(2):
        for row, z in jobs:
            tiles = [rows_ref[f, t, z + RIM : z + RIM + GROUP, :] for t in range(blocks)]
            across = lateral(tiles, lane)
            out = []
            for t in range(blocks):
                at = slice(t * LANES, (t + 1) * LANES)
                total = (2.0 * coeffs[0]) * tiles[t] + across[t]
                for k in range(1, RIM + 1):
                    total = total + coeffs[k] * (
                        rows_ref[f, t, z + RIM - k : z + RIM - k + GROUP, :] + rows_ref[f, t, z + RIM + k : z + RIM + k + GROUP, :]
                    )
                value = 2.0 * tiles[t] - prevs[f][0, z : z + GROUP, at] + courant[z : z + GROUP, at] * total
                if f == 0:
                    value = value + jnp.where(flat == cell - (z * nx + t * LANES), amp, 0.0)
                out.append(value)
            if f == 0:
                turned = jnp.dot(
                    jnp.concatenate(out[::-1], 0), mirror, precision=lax.Precision.HIGHEST, preferred_element_type=jnp.float32
                )
                out = [turned[t * GROUP : (t + 1) * GROUP, :] for t in range(blocks)]
            else:
                out = [pltpu.roll(v, MAXLAG, 1) for v in out]
            out = [zero] + out + [zero]
            for t in range(blocks + 1):
                padded[f, row : row + GROUP, t * LANES : (t + 1) * LANES] = jnp.where(half, out[t], out[t + 1])
    for d, out in enumerate(outs):
        other = lax.bitwise_xor(me, d)
        for f, first in enumerate((count - 1 - other, other)):
            out[f] = padded[f, :, pl.ds(pl.multiple_of(first * width, LANES), width + 2 * MAXLAG)]


def inner_body(width, cell_ref, amp_ref, src_now, src_prev, rcv_now, rcv_prev, courant, up_ref, down_ref, *refs):
    outs, rows_ref, padded = refs[:-2], refs[-2], refs[-1]
    depth, nx = src_now.shape[1:]
    for f, now in enumerate((src_now, rcv_now)):
        up_ref[f * RIM : (f + 1) * RIM, :] = now[0, 0:RIM, :]
        down_ref[f * RIM : (f + 1) * RIM, :] = now[0, depth - RIM : depth, :]
        for t in range(nx // LANES):
            rows_ref[f, t, RIM : RIM + depth, :] = now[0, :, t * LANES : (t + 1) * LANES]
    jobs = [(z - GROUP, z) for z in range(GROUP, depth - GROUP, GROUP)]
    step_rows(jobs, width, cell_ref, amp_ref, (src_prev, rcv_prev), courant, rows_ref, padded, outs)


def outer_body(width, cell_ref, amp_ref, above, below, src_now, src_prev, rcv_now, rcv_prev, courant, *refs):
    outs, rows_ref, padded = refs[:-2], refs[-2], refs[-1]
    depth, nx = src_now.shape[1:]
    for f, now in enumerate((src_now, rcv_now)):
        for t in range(nx // LANES):
            at = slice(t * LANES, (t + 1) * LANES)
            rows_ref[f, t, 0:RIM, :] = above[f * RIM : (f + 1) * RIM, at]
            rows_ref[f, t, RIM : RIM + 2 * GROUP, :] = now[0, 0 : 2 * GROUP, at]
            rows_ref[f, t, RIM + depth - 2 * GROUP : RIM + depth, :] = now[0, depth - 2 * GROUP : depth, at]
            rows_ref[f, t, RIM + depth : 2 * RIM + depth, :] = below[f * RIM : (f + 1) * RIM, at]
    jobs = [(0, 0), (GROUP, depth - GROUP)]
    step_rows(jobs, width, cell_ref, amp_ref, (src_prev, rcv_prev), courant, rows_ref, padded, outs)


def windows(body, name, count, rows, halos, extra, cell, amp, fields):
    depth, nx = fields[0].shape[1:]
    width = nx // count
    out = jax.ShapeDtypeStruct((2, rows, width + 2 * MAXLAG), jnp.float32)
    smem = pl.BlockSpec(memory_space=pltpu.SMEM)
    vmem = pl.BlockSpec(memory_space=pltpu.VMEM)
    return pl.pallas_call(
        functools.partial(body, width),
        in_specs=[smem, smem] + [vmem] * (len(halos) + len(fields)),
        out_specs=[vmem] * (len(extra) + count),
        out_shape=extra + [out] * count,
        scratch_shapes=[
            pltpu.VMEM((2, nx // LANES, depth + 2 * RIM, LANES), jnp.float32),
            pltpu.VMEM((2, rows, nx + 2 * MAXLAG), jnp.float32),
        ],
        name=name,
    )(cell, amp, *halos, *fields)


def weight_body(shift_ref, map_ref, mw_ref, slot_ref):
    lag = lax.broadcasted_iota(jnp.int32, (ROWS, LANES), 0) - MAXLAG
    hot = jnp.where(lag == shift_ref[...], 1.0, 0.0)
    full = lax.dot_general(
        map_ref[...], hot, (((1,), (1,)), ((), ())), precision=lax.Precision.HIGHEST, preferred_element_type=jnp.float32
    )
    na = full.shape[0]
    used = jnp.max(hot[:LANES, :], axis=1, keepdims=True)
    k = lax.broadcasted_iota(jnp.int32, (LANES, 1), 0).astype(jnp.float32)
    slot = jnp.min(jnp.where(used > 0.0, float(ROWS), k), axis=0, keepdims=True).astype(jnp.int32)
    column = lax.broadcasted_iota(jnp.int32, (na, LANES), 1)
    w = jnp.where(column == slot, full[:, LANES : LANES + 1], full[:, :LANES])
    high, low = split(w)
    mw_ref[0, :, :LANES] = high
    mw_ref[0, :, LANES:] = high
    mw_ref[1, :, :LANES] = low
    mw_ref[1, :, LANES:] = jnp.zeros_like(low)
    slot_ref[...] = jnp.broadcast_to(slot, slot_ref.shape)


def angle_weights(shifts, angle_map):
    na = angle_map.shape[0]
    return pl.pallas_call(
        weight_body,
        out_shape=[jax.ShapeDtypeStruct((2, na, ROWS), jnp.bfloat16), jax.ShapeDtypeStruct((GROUP, LANES), jnp.int32)],
        name="angle_weights",
    )(shifts.reshape(1, -1), angle_map)


def products(na, shots, slot_ref, mw_ref, fwd, rev, obuf, rhs):
    slot = slot_ref[...]
    sub = lax.broadcasted_iota(jnp.int32, (GROUP, LANES), 0)
    steps = 16 // MB

    def fill(rho, mb, buf):
        extra = []
        for m in range(mb * MB, (mb + 1) * MB):
            tot = None
            for s in range(shots):
                t = rev[s, pl.ds(ROWS - 1 - 8 * m - rho, 1), :] * fwd[s, pl.ds(LANES + 8 * m + rho, 1), :]
                tot = t if tot is None else tot + t
            extra.append(jnp.broadcast_to(tot, (GROUP, LANES)))
        for nb in range(16 // NB):
            acc = [[None] * NB for _ in range(MB)]
            for s in range(shots):
                a = {}
                c = {}
                for i in range(MB):
                    for j in range(NB):
                        m, n = mb * MB + i, nb * NB + j
                        if n - m not in a:
                            a[n - m] = rev[s, pl.ds(LANES - 1 - rho + 8 * (n - m), GROUP), :]
                        if n + m not in c:
                            c[n + m] = fwd[s, pl.ds(rho + 8 * (n + m), GROUP), :]
                        t = a[n - m] * c[n + m]
                        acc[i][j] = t if acc[i][j] is None else acc[i][j] + t
            for j in range(0, NB, 2):
                n = nb * NB + j
                masks = [sub == slot - 8 * (n + k) for k in range(2)]
                for i in range(MB):
                    high, low = split(jnp.concatenate([jnp.where(masks[k], extra[i], acc[i][j + k]) for k in range(2)], 0))
                    rhs[buf, 8 * n : 8 * n + 16, i * LANES : (i + 1) * LANES] = high
                    rhs[buf, LANES + 8 * n : LANES + 8 * n + 16, i * LANES : (i + 1) * LANES] = low

    def contract(rho, mb, buf):
        res = jnp.dot(mw_ref[0], rhs[buf], preferred_element_type=jnp.float32)
        res += jnp.dot(mw_ref[1], rhs[buf], preferred_element_type=jnp.float32)
        for i in range(MB):
            obuf[pl.ds(8 * (mb * MB + i) + rho, na, stride=PITCH), :] = res[:, i * LANES : (i + 1) * LANES]

    items = [(rho, mb) for rho in range(GROUP) for mb in range(steps)]
    for i, (rho, mb) in enumerate(items):
        fill(rho, mb, i % 2)
        if i:
            contract(*items[i - 1], (i - 1) % 2)
    contract(*items[-1], (len(items) - 1) % 2)


def image_body(blocks, shots, slot_ref, mw_ref, *refs):
    sent = refs[: 2 * shots]
    out_ref, held, fwd, rev, obuf, stage, in_sems, out_sems = refs[2 * shots :]
    na, depth, _ = out_ref.shape
    fetches = [pltpu.make_async_copy(sent[i], held.at[i], in_sems.at[i]) for i in range(2 * shots)]
    for fetch in fetches:
        fetch.start()

    def gathered(s, f, b):
        inner, outer = held.at[s], held.at[shots + s]
        tiles = []
        for q in range(blocks):
            t = q + b if f else blocks - 1 - q + b
            at = slice(t * LANES, (t + 1) * LANES)
            tiles += [outer[f, :GROUP, at], inner[f, :, at], outer[f, GROUP:, at]]
        if blocks * depth < LANES:
            tiles.append(jnp.zeros((LANES - blocks * depth, LANES), jnp.float32))
        return jnp.concatenate(tiles, 0)

    for fetch in fetches:
        fetch.wait()
    for s in range(shots):
        for b in range(2):
            fwd[s, b * LANES : (b + 1) * LANES, :] = gathered(s, 1, b).T
            rev[s, b * LANES : (b + 1) * LANES, :] = gathered(s, 0, b).T

    pl.run_scoped(
        functools.partial(products, na, shots, slot_ref, mw_ref, fwd, rev, obuf),
        pltpu.VMEM((2, ROWS, LANES * MB), jnp.bfloat16),
    )

    def leave(i):
        at = pl.ds(i * APART, APART)
        return pltpu.make_async_copy(stage.at[at], out_ref.at[at], out_sems.at[i])

    @pl.loop(0, na // (2 * APART))
    def _(i):
        for part in range(2):
            for a in range(APART):
                angle = (2 * i + part) * APART + a
                tile = obuf[pl.ds(angle * PITCH, LANES), :].T
                for q in range(blocks):
                    stage[angle, :, q * LANES : (q + 1) * LANES] = tile[q * depth : (q + 1) * depth, :]
            leave(2 * i + part).start()

    @pl.loop(0, na // APART)
    def _(i):
        leave(i).wait()


def angle_image(inner, outer, mw, slot, depth):
    shots = len(inner)
    full = inner[0].shape[2]
    width = full - 2 * MAXLAG
    na = mw.shape[1]
    vmem = pl.BlockSpec(memory_space=pltpu.VMEM)
    anywhere = pl.BlockSpec(memory_space=pl.ANY)
    return pl.pallas_call(
        functools.partial(image_body, width // LANES, shots),
        out_shape=jax.ShapeDtypeStruct((na, depth, width), jnp.float32),
        in_specs=[vmem, vmem] + [anywhere] * (2 * shots),
        out_specs=anywhere,
        scratch_shapes=[
            pltpu.VMEM((2 * shots, *inner[0].shape), jnp.float32),
            pltpu.VMEM((shots, ROWS, LANES), jnp.float32),
            pltpu.VMEM((shots, ROWS, LANES), jnp.float32),
            pltpu.VMEM((na * PITCH, LANES), jnp.float32),
            pltpu.VMEM((na, depth, width), jnp.float32),
            pltpu.SemaphoreType.DMA((2 * shots,)),
            pltpu.SemaphoreType.DMA((na // APART,)),
        ],
        compiler_params=pltpu.CompilerParams(vmem_limit_bytes=40 << 20),
        name="angle_image",
    )(slot, mw, *inner, *outer)


def body(src_now, src_prev, rcv_now, rcv_prev, courant, shot_cell, wavelet, shifts, angle_map):
    depth = src_now.shape[1]
    count = lax.axis_size("offset")
    slabs = lax.axis_size("space")
    fields = (src_now, src_prev, rcv_now, rcv_prev, courant)
    edge = jax.ShapeDtypeStruct((2 * RIM, src_now.shape[2]), jnp.float32)

    def exchanged(wins):
        return [wins[0]] + [lax.ppermute(wins[d], "offset", [(i, i ^ d) for i in range(count)]) for d in range(1, count)]

    up, down, *inner = windows(
        inner_body, "inner_rows", count, depth - 2 * GROUP, (), [edge, edge], shot_cell, wavelet, fields
    )
    below = lax.ppermute(up, "space", [(i + 1, i) for i in range(slabs - 1)])
    above = lax.ppermute(down, "space", [(i, i + 1) for i in range(slabs - 1)])
    inner = exchanged(inner)
    outer = exchanged(windows(outer_body, "outer_rows", count, 2 * GROUP, (above, below), [], shot_cell, wavelet, fields))
    mw, slot = angle_weights(shifts, angle_map)
    return angle_image(inner, outer, mw, slot, depth)


def solution(mesh):
    placed = (
        P("offset", ("groups", "space"), None),
        P("offset", ("groups", "space"), None),
        P("offset", ("groups", "space"), None),
        P("offset", ("groups", "space"), None),
        P(("groups", "space"), None),
        P("groups"),
        P("groups"),
        P(),
        P(),
    )
    step = jax.shard_map(
        body,
        mesh=mesh,
        in_specs=placed,
        out_specs=P(None, ("groups", "space"), "offset"),
        check_vma=False,
    )

    def run(*args):
        with jax.sharding.use_abstract_mesh(mesh.abstract_mesh):
            return step(*args)

    return run
```

```python
import functools

import jax
import jax.numpy as jnp
from jax import lax
from jax.experimental import pallas as pl
from jax.experimental.pallas import tpu as pltpu
from jax.sharding import PartitionSpec as P

MAXLAG = 64
LANES = 128
ROWS = 2 * LANES
GROUP = 8
RIM = 4
PITCH = LANES + 1
MB = 4
NB = 4
APART = 16

coeffs = (-205.0 / 72.0, 8.0 / 5.0, -1.0 / 5.0, 8.0 / 315.0, -1.0 / 560.0)


def split(x):
    high = x.astype(jnp.bfloat16)
    low = (x - high.astype(jnp.float32)).astype(jnp.bfloat16)
    return high, low


def lateral(tiles, lane):
    zero = jnp.zeros_like(tiles[0])
    total = [None] * len(tiles)
    for k in range(1, RIM + 1):
        up = [pltpu.roll(v, k, 1) for v in tiles]
        down = [pltpu.roll(v, LANES - k, 1) for v in tiles]
        for t in range(len(tiles)):
            left = jnp.where(lane < k, up[t - 1] if t else zero, up[t])
            right = jnp.where(lane >= LANES - k, down[t + 1] if t + 1 < len(tiles) else zero, down[t])
            term = coeffs[k] * (left + right)
            total[t] = term if total[t] is None else total[t] + term
    return total


def step_rows(jobs, width, cell_ref, amp_ref, prevs, courant, rows_ref, padded, outs):
    pitch = rows_ref.shape[2]
    count = len(outs)
    nx = courant.shape[1]
    depth = courant.shape[0]
    blocks = nx // LANES
    me = lax.axis_index("offset")
    cell = cell_ref[me] - lax.axis_index("space") * depth * nx
    amp = amp_ref[me]
    lane = lax.broadcasted_iota(jnp.int32, (GROUP, LANES), 1)
    flat = lax.broadcasted_iota(jnp.int32, (GROUP, LANES), 0) * nx + lane
    source = lax.broadcasted_iota(jnp.int32, (LANES, LANES), 0)
    target = lax.broadcasted_iota(jnp.int32, (LANES, LANES), 1)
    mirror = (lax.rem(source + target + 1, LANES) == MAXLAG).astype(jnp.float32)
    half = lane < MAXLAG
    zero = jnp.zeros((GROUP, LANES), jnp.float32)
    for f in range(2):
        for row, z in jobs:
            tiles = [rows_ref[f, t, z + RIM : z + RIM + GROUP, :] for t in range(blocks)]
            across = lateral(tiles, lane)
            out = []
            for t in range(blocks):
                at = slice(t * LANES, (t + 1) * LANES)
                total = (2.0 * coeffs[0]) * tiles[t] + across[t]
                for k in range(1, RIM + 1):
                    total = total + coeffs[k] * (
                        rows_ref[f, t, z + RIM - k : z + RIM - k + GROUP, :] + rows_ref[f, t, z + RIM + k : z + RIM + k + GROUP, :]
                    )
                value = 2.0 * tiles[t] - prevs[f][0, z : z + GROUP, at] + courant[z : z + GROUP, at] * total
                if f == 0:
                    value = value + jnp.where(flat == cell - (z * nx + t * LANES), amp, 0.0)
                out.append(value)
            if f == 0:
                turned = jnp.dot(
                    jnp.concatenate(out[::-1], 0), mirror, precision=lax.Precision.HIGHEST, preferred_element_type=jnp.float32
                )
                out = [turned[t * GROUP : (t + 1) * GROUP, :] for t in range(blocks)]
            else:
                out = [pltpu.roll(v, MAXLAG, 1) for v in out]
            out = [zero] + out + [zero]
            for t in range(blocks + 1):
                padded[f, row : row + GROUP, t * LANES : (t + 1) * LANES] = jnp.where(half, out[t], out[t + 1])
    for d, out in enumerate(outs):
        other = lax.bitwise_xor(me, d)
        for f, first in enumerate((count - 1 - other, other)):
            out[f] = padded[f, :, pl.ds(pl.multiple_of(first * width, LANES), width + 2 * MAXLAG)]


def inner_body(width, cell_ref, amp_ref, src_now, src_prev, rcv_now, rcv_prev, courant, up_ref, down_ref, *refs):
    outs, rows_ref, padded = refs[:-2], refs[-2], refs[-1]
    depth, nx = src_now.shape[1:]
    for f, now in enumerate((src_now, rcv_now)):
        up_ref[f * RIM : (f + 1) * RIM, :] = now[0, 0:RIM, :]
        down_ref[f * RIM : (f + 1) * RIM, :] = now[0, depth - RIM : depth, :]
        for t in range(nx // LANES):
            rows_ref[f, t, RIM : RIM + depth, :] = now[0, :, t * LANES : (t + 1) * LANES]
    jobs = [(z - GROUP, z) for z in range(GROUP, depth - GROUP, GROUP)]
    step_rows(jobs, width, cell_ref, amp_ref, (src_prev, rcv_prev), courant, rows_ref, padded, outs)


def outer_body(width, cell_ref, amp_ref, above, below, src_now, src_prev, rcv_now, rcv_prev, courant, *refs):
    outs, rows_ref, padded = refs[:-2], refs[-2], refs[-1]
    depth, nx = src_now.shape[1:]
    for f, now in enumerate((src_now, rcv_now)):
        for t in range(nx // LANES):
            at = slice(t * LANES, (t + 1) * LANES)
            rows_ref[f, t, 0:RIM, :] = above[f * RIM : (f + 1) * RIM, at]
            rows_ref[f, t, RIM : RIM + 2 * GROUP, :] = now[0, 0 : 2 * GROUP, at]
            rows_ref[f, t, RIM + depth - 2 * GROUP : RIM + depth, :] = now[0, depth - 2 * GROUP : depth, at]
            rows_ref[f, t, RIM + depth : 2 * RIM + depth, :] = below[f * RIM : (f + 1) * RIM, at]
    jobs = [(0, 0), (GROUP, depth - GROUP)]
    step_rows(jobs, width, cell_ref, amp_ref, (src_prev, rcv_prev), courant, rows_ref, padded, outs)


def windows(body, name, count, rows, halos, extra, cell, amp, fields):
    depth, nx = fields[0].shape[1:]
    width = nx // count
    out = jax.ShapeDtypeStruct((2, rows, width + 2 * MAXLAG), jnp.float32)
    smem = pl.BlockSpec(memory_space=pltpu.SMEM)
    vmem = pl.BlockSpec(memory_space=pltpu.VMEM)
    return pl.pallas_call(
        functools.partial(body, width),
        in_specs=[smem, smem] + [vmem] * (len(halos) + len(fields)),
        out_specs=[vmem] * (len(extra) + count),
        out_shape=extra + [out] * count,
        scratch_shapes=[
            pltpu.VMEM((2, nx // LANES, depth + 2 * RIM, LANES), jnp.float32),
            pltpu.VMEM((2, rows, nx + 2 * MAXLAG), jnp.float32),
        ],
        compiler_params=pltpu.CompilerParams(vmem_limit_bytes=60 << 20),
        name=name,
    )(cell, amp, *halos, *fields)


def weight_body(shift_ref, map_ref, mw_ref, slot_ref):
    lag = lax.broadcasted_iota(jnp.int32, (ROWS, LANES), 0) - MAXLAG
    hot = jnp.where(lag == shift_ref[...], 1.0, 0.0)
    full = lax.dot_general(
        map_ref[...], hot, (((1,), (1,)), ((), ())), precision=lax.Precision.HIGHEST, preferred_element_type=jnp.float32
    )
    na = full.shape[0]
    used = jnp.max(hot[:LANES, :], axis=1, keepdims=True)
    k = lax.broadcasted_iota(jnp.int32, (LANES, 1), 0).astype(jnp.float32)
    slot = jnp.min(jnp.where(used > 0.0, float(ROWS), k), axis=0, keepdims=True).astype(jnp.int32)
    column = lax.broadcasted_iota(jnp.int32, (na, LANES), 1)
    w = jnp.where(column == slot, full[:, LANES : LANES + 1], full[:, :LANES])
    high, low = split(w)
    mw_ref[0, :, :LANES] = high
    mw_ref[0, :, LANES:] = high
    mw_ref[1, :, :LANES] = low
    mw_ref[1, :, LANES:] = jnp.zeros_like(low)
    slot_ref[...] = jnp.broadcast_to(slot, slot_ref.shape)


def angle_weights(shifts, angle_map):
    na = angle_map.shape[0]
    return pl.pallas_call(
        weight_body,
        out_shape=[jax.ShapeDtypeStruct((2, na, ROWS), jnp.bfloat16), jax.ShapeDtypeStruct((GROUP, LANES), jnp.int32)],
        compiler_params=pltpu.CompilerParams(vmem_limit_bytes=60 << 20),
        name="angle_weights",
    )(shifts.reshape(1, -1), angle_map)


def products(na, shots, slot_ref, mw_ref, fwd, rev, obuf, rhs):
    slot = slot_ref[...]
    sub = lax.broadcasted_iota(jnp.int32, (GROUP, LANES), 0)
    steps = 16 // MB

    def fill(rho, mb, buf):
        extra = []
        for m in range(mb * MB, (mb + 1) * MB):
            tot = None
            for s in range(shots):
                t = rev[s, pl.ds(ROWS - 1 - 8 * m - rho, 1), :] * fwd[s, pl.ds(LANES + 8 * m + rho, 1), :]
                tot = t if tot is None else tot + t
            extra.append(jnp.broadcast_to(tot, (GROUP, LANES)))
        for nb in range(16 // NB):
            acc = [[None] * NB for _ in range(MB)]
            for s in range(shots):
                a = {}
                c = {}
                for i in range(MB):
                    for j in range(NB):
                        m, n = mb * MB + i, nb * NB + j
                        if n - m not in a:
                            a[n - m] = rev[s, pl.ds(LANES - 1 - rho + 8 * (n - m), GROUP), :]
                        if n + m not in c:
                            c[n + m] = fwd[s, pl.ds(rho + 8 * (n + m), GROUP), :]
                        t = a[n - m] * c[n + m]
                        acc[i][j] = t if acc[i][j] is None else acc[i][j] + t
            for j in range(0, NB, 2):
                n = nb * NB + j
                masks = [sub == slot - 8 * (n + k) for k in range(2)]
                for i in range(MB):
                    high, low = split(jnp.concatenate([jnp.where(masks[k], extra[i], acc[i][j + k]) for k in range(2)], 0))
                    rhs[buf, 8 * n : 8 * n + 16, i * LANES : (i + 1) * LANES] = high
                    rhs[buf, LANES + 8 * n : LANES + 8 * n + 16, i * LANES : (i + 1) * LANES] = low

    def contract(rho, mb, buf):
        res = jnp.dot(mw_ref[0], rhs[buf], preferred_element_type=jnp.float32)
        res += jnp.dot(mw_ref[1], rhs[buf], preferred_element_type=jnp.float32)
        for i in range(MB):
            obuf[pl.ds(8 * (mb * MB + i) + rho, na, stride=PITCH), :] = res[:, i * LANES : (i + 1) * LANES]

    def turn(rhos):
        items = [(rho, mb) for rho in rhos for mb in range(steps)]
        for i, (rho, mb) in enumerate(items):
            fill(rho, mb, i % 2)
            if i:
                contract(*items[i - 1], (i - 1) % 2)
        contract(*items[-1], (len(items) - 1) % 2)

    if shots <= 4:
        turn(range(GROUP))
    else:

        @pl.loop(0, GROUP)
        def _(rho):
            turn([rho])


def image_body(blocks, shots, slot_hbm, mw_hbm, *refs):
    sent = refs[: 2 * shots]
    out_ref, slot_ref, mw_ref, held, fwd, rev, obuf, stage, in_sems, out_sems = refs[2 * shots :]
    na, depth, _ = out_ref.shape
    fetches = [pltpu.make_async_copy(sent[i], held.at[i], in_sems.at[i]) for i in range(2 * shots)]
    fetches.append(pltpu.make_async_copy(slot_hbm, slot_ref, in_sems.at[2 * shots]))
    fetches.append(pltpu.make_async_copy(mw_hbm, mw_ref, in_sems.at[2 * shots + 1]))
    for fetch in fetches:
        fetch.start()

    def gathered(s, f, b):
        inner, outer = held.at[s], held.at[shots + s]
        tiles = []
        for q in range(blocks):
            t = q + b if f else blocks - 1 - q + b
            at = slice(t * LANES, (t + 1) * LANES)
            tiles += [outer[f, :GROUP, at], inner[f, :, at], outer[f, GROUP:, at]]
        if blocks * depth < LANES:
            tiles.append(jnp.zeros((LANES - blocks * depth, LANES), jnp.float32))
        return jnp.concatenate(tiles, 0)

    for fetch in fetches:
        fetch.wait()
    for s in range(shots):
        for b in range(2):
            fwd[s, b * LANES : (b + 1) * LANES, :] = gathered(s, 1, b).T
            rev[s, b * LANES : (b + 1) * LANES, :] = gathered(s, 0, b).T

    pl.run_scoped(
        functools.partial(products, na, shots, slot_ref, mw_ref, fwd, rev, obuf),
        pltpu.VMEM((2, ROWS, LANES * MB), jnp.bfloat16),
    )

    def leave(i):
        at = pl.ds(i * APART, APART)
        return pltpu.make_async_copy(stage.at[at], out_ref.at[at], out_sems.at[i])

    @pl.loop(0, na // (2 * APART))
    def _(i):
        for part in range(2):
            for a in range(APART):
                angle = (2 * i + part) * APART + a
                tile = obuf[pl.ds(angle * PITCH, LANES), :].T
                for q in range(blocks):
                    stage[angle, :, q * LANES : (q + 1) * LANES] = tile[q * depth : (q + 1) * depth, :]
            leave(2 * i + part).start()

    @pl.loop(0, na // APART)
    def _(i):
        leave(i).wait()


def angle_image(inner, outer, mw, slot, depth):
    shots = len(inner)
    full = inner[0].shape[2]
    width = full - 2 * MAXLAG
    na = mw.shape[1]
    anywhere = pl.BlockSpec(memory_space=pl.ANY)
    return pl.pallas_call(
        functools.partial(image_body, width // LANES, shots),
        out_shape=jax.ShapeDtypeStruct((na, depth, width), jnp.float32),
        in_specs=[anywhere] * (2 + 2 * shots),
        out_specs=pl.BlockSpec(memory_space=pltpu.HBM),
        scratch_shapes=[
            pltpu.VMEM(slot.shape, slot.dtype),
            pltpu.VMEM(mw.shape, mw.dtype),
            pltpu.VMEM((2 * shots, *inner[0].shape), jnp.float32),
            pltpu.VMEM((shots, ROWS, LANES), jnp.float32),
            pltpu.VMEM((shots, ROWS, LANES), jnp.float32),
            pltpu.VMEM((na * PITCH, LANES), jnp.float32),
            pltpu.VMEM((na, depth, width), jnp.float32),
            pltpu.SemaphoreType.DMA((2 * shots + 2,)),
            pltpu.SemaphoreType.DMA((na // APART,)),
        ],
        compiler_params=pltpu.CompilerParams(vmem_limit_bytes=60 << 20),
        name="angle_image",
    )(slot, mw, *inner, *outer)


def body(src_now, src_prev, rcv_now, rcv_prev, courant, shot_cell, wavelet, shifts, angle_map):
    depth = src_now.shape[1]
    count = lax.axis_size("offset")
    slabs = lax.axis_size("space")
    fields = (src_now, src_prev, rcv_now, rcv_prev, courant)
    edge = jax.ShapeDtypeStruct((2 * RIM, src_now.shape[2]), jnp.float32)

    def exchanged(wins):
        return [wins[0]] + [lax.ppermute(wins[d], "offset", [(i, i ^ d) for i in range(count)]) for d in range(1, count)]

    up, down, *inner = windows(
        inner_body, "inner_rows", count, depth - 2 * GROUP, (), [edge, edge], shot_cell, wavelet, fields
    )
    below = lax.ppermute(up, "space", [(i + 1, i) for i in range(slabs - 1)])
    above = lax.ppermute(down, "space", [(i, i + 1) for i in range(slabs - 1)])
    inner = exchanged(inner)
    outer = exchanged(windows(outer_body, "outer_rows", count, 2 * GROUP, (above, below), [], shot_cell, wavelet, fields))
    mw, slot = angle_weights(shifts, angle_map)
    return angle_image(inner, outer, mw, slot, depth)


def solution(mesh):
    placed = (
        P("offset", ("groups", "space"), None),
        P("offset", ("groups", "space"), None),
        P("offset", ("groups", "space"), None),
        P("offset", ("groups", "space"), None),
        P(("groups", "space"), None),
        P("groups"),
        P("groups"),
        P(),
        P(),
    )
    step = jax.shard_map(
        body,
        mesh=mesh,
        in_specs=placed,
        out_specs=P(None, ("groups", "space"), "offset"),
        check_vma=False,
    )

    def run(*args):
        with jax.sharding.use_abstract_mesh(mesh.abstract_mesh):
            return step(*args)

    return run
```

```python
import functools

import jax
import jax.numpy as jnp
from jax import lax
from jax.experimental import pallas as pl
from jax.experimental.pallas import tpu as pltpu
from jax.sharding import PartitionSpec as P

MAXLAG = 64
LANES = 128
ROWS = 2 * LANES
GROUP = 8
RIM = 4
PITCH = LANES + 1
MB = 4
NB = 4
APART = 16

coeffs = (-205.0 / 72.0, 8.0 / 5.0, -1.0 / 5.0, 8.0 / 315.0, -1.0 / 560.0)


def split(x):
    high = x.astype(jnp.bfloat16)
    low = (x - high.astype(jnp.float32)).astype(jnp.bfloat16)
    return high, low


def lateral(tiles, lane):
    zero = jnp.zeros_like(tiles[0])
    total = [None] * len(tiles)
    for k in range(1, RIM + 1):
        up = [pltpu.roll(v, k, 1) for v in tiles]
        down = [pltpu.roll(v, LANES - k, 1) for v in tiles]
        for t in range(len(tiles)):
            left = jnp.where(lane < k, up[t - 1] if t else zero, up[t])
            right = jnp.where(lane >= LANES - k, down[t + 1] if t + 1 < len(tiles) else zero, down[t])
            term = coeffs[k] * (left + right)
            total[t] = term if total[t] is None else total[t] + term
    return total


def step_body(width, cell_ref, amp_ref, src_now, src_prev, rcv_now, rcv_prev, courant, speed_ref, *refs):
    count = (len(refs) - 4) // 2
    rims, wins = refs[:count], refs[count : 2 * count]
    rows_ref, padded, padded_rim, padded_speed = refs[2 * count :]
    depth, nx = src_now.shape[1:]
    blocks = nx // LANES
    me = lax.axis_index("offset")
    cell = cell_ref[me] - lax.axis_index("space") * depth * nx
    amp = amp_ref[me]
    lane = lax.broadcasted_iota(jnp.int32, (GROUP, LANES), 1)
    flat = lax.broadcasted_iota(jnp.int32, (GROUP, LANES), 0) * nx + lane
    source = lax.broadcasted_iota(jnp.int32, (LANES, LANES), 0)
    target = lax.broadcasted_iota(jnp.int32, (LANES, LANES), 1)
    mirror = (lax.rem(source + target + 1, LANES) == MAXLAG).astype(jnp.float32)
    half = lane < MAXLAG
    zero = jnp.zeros((GROUP, LANES), jnp.float32)

    def place(ref, f, row, out):
        if f == 0:
            turned = jnp.dot(
                jnp.concatenate(out[::-1], 0), mirror, precision=lax.Precision.HIGHEST, preferred_element_type=jnp.float32
            )
            out = [turned[t * GROUP : (t + 1) * GROUP, :] for t in range(blocks)]
        else:
            out = [pltpu.roll(v, MAXLAG, 1) for v in out]
        out = [zero] + out + [zero]
        for t in range(blocks + 1):
            ref[f, row : row + GROUP, t * LANES : (t + 1) * LANES] = jnp.where(half, out[t], out[t + 1])

    cuts = [slice(t * LANES, (t + 1) * LANES) for t in range(blocks)]
    nows, prevs = (src_now, rcv_now), (src_prev, rcv_prev)
    for f in range(2):
        now = nows[f]
        place(padded_rim, f, 0, [jnp.concatenate([now[0, :RIM, at], now[0, depth - RIM :, at]], 0) for at in cuts])
        for b, z in enumerate((0, depth - GROUP)):
            place(padded_speed, f, b * GROUP, [courant[z : z + GROUP, at] for at in cuts])
        for t in range(blocks):
            rows_ref[f, t, 0:GROUP, :] = zero
            rows_ref[f, t, GROUP : GROUP + depth, :] = now[0, :, cuts[t]]
            rows_ref[f, t, GROUP + depth : 2 * GROUP + depth, :] = zero
        for z in range(0, depth, GROUP):
            at = z + GROUP
            tiles = [rows_ref[f, t, at : at + GROUP, :] for t in range(blocks)]
            across = lateral(tiles, lane)
            out = []
            for t in range(blocks):
                total = (2.0 * coeffs[0]) * tiles[t] + across[t]
                for k in range(1, RIM + 1):
                    total = total + coeffs[k] * (rows_ref[f, t, at - k : at - k + GROUP, :] + rows_ref[f, t, at + k : at + k + GROUP, :])
                value = 2.0 * tiles[t] - prevs[f][0, z : z + GROUP, cuts[t]] + courant[z : z + GROUP, cuts[t]] * total
                if f == 0:
                    value = value + jnp.where(flat == cell - (z * nx + t * LANES), amp, 0.0)
                out.append(value)
            place(padded, f, z, out)
    for d in range(count):
        other = lax.bitwise_xor(me, d)
        for f, first in enumerate((count - 1 - other, other)):
            at = pl.ds(pl.multiple_of(first * width, LANES), width + 2 * MAXLAG)
            rims[d][f] = padded_rim[f, :, at]
            wins[d][f] = padded[f, :, at]
            if d == 0:
                speed_ref[f] = padded_speed[f, :, at]


def stepped_windows(count, cell, amp, fields):
    depth, nx = fields[0].shape[1:]
    width = nx // count
    shape = lambda rows: jax.ShapeDtypeStruct((2, rows, width + 2 * MAXLAG), jnp.float32)
    smem = pl.BlockSpec(memory_space=pltpu.SMEM)
    vmem = pl.BlockSpec(memory_space=pltpu.VMEM)
    speed, *rest = pl.pallas_call(
        functools.partial(step_body, width),
        in_specs=[smem, smem] + [vmem] * len(fields),
        out_specs=[vmem] * (1 + 2 * count),
        out_shape=[shape(2 * GROUP)] + [shape(GROUP)] * count + [shape(depth)] * count,
        scratch_shapes=[
            pltpu.VMEM((2, nx // LANES, depth + 2 * GROUP, LANES), jnp.float32),
            pltpu.VMEM((2, depth, nx + 2 * MAXLAG), jnp.float32),
            pltpu.VMEM((2, GROUP, nx + 2 * MAXLAG), jnp.float32),
            pltpu.VMEM((2, 2 * GROUP, nx + 2 * MAXLAG), jnp.float32),
        ],
        compiler_params=pltpu.CompilerParams(vmem_limit_bytes=60 << 20),
        name="step",
    )(cell, amp, *fields)
    return speed, rest[:count], rest[count:]


def rim_body(*refs):
    shots = len(refs) - 2
    up_ref, down_ref = refs[shots:]
    for s in range(shots):
        for f in range(2):
            up_ref[s, f * RIM : (f + 1) * RIM, :] = refs[s][f, :RIM, :]
            down_ref[s, f * RIM : (f + 1) * RIM, :] = refs[s][f, RIM:, :]


def rims_by_side(rims):
    out = jax.ShapeDtypeStruct((len(rims), 2 * RIM, rims[0].shape[2]), jnp.float32)
    return pl.pallas_call(
        rim_body,
        out_shape=[out, out],
        compiler_params=pltpu.CompilerParams(vmem_limit_bytes=60 << 20),
        name="rims_by_side",
    )(*rims)


def weight_body(shift_ref, map_ref, mw_ref, slot_ref):
    lag = lax.broadcasted_iota(jnp.int32, (ROWS, LANES), 0) - MAXLAG
    hot = jnp.where(lag == shift_ref[...], 1.0, 0.0)
    full = lax.dot_general(
        map_ref[...], hot, (((1,), (1,)), ((), ())), precision=lax.Precision.HIGHEST, preferred_element_type=jnp.float32
    )
    na = full.shape[0]
    used = jnp.max(hot[:LANES, :], axis=1, keepdims=True)
    k = lax.broadcasted_iota(jnp.int32, (LANES, 1), 0).astype(jnp.float32)
    slot = jnp.min(jnp.where(used > 0.0, float(ROWS), k), axis=0, keepdims=True).astype(jnp.int32)
    column = lax.broadcasted_iota(jnp.int32, (na, LANES), 1)
    w = jnp.where(column == slot, full[:, LANES : LANES + 1], full[:, :LANES])
    high, low = split(w)
    mw_ref[0, :, :LANES] = high
    mw_ref[0, :, LANES:] = high
    mw_ref[1, :, :LANES] = low
    mw_ref[1, :, LANES:] = jnp.zeros_like(low)
    slot_ref[...] = jnp.broadcast_to(slot, slot_ref.shape)


def angle_weights(shifts, angle_map):
    na = angle_map.shape[0]
    return pl.pallas_call(
        weight_body,
        out_shape=[jax.ShapeDtypeStruct((2, na, ROWS), jnp.bfloat16), jax.ShapeDtypeStruct((GROUP, LANES), jnp.int32)],
        compiler_params=pltpu.CompilerParams(vmem_limit_bytes=60 << 20),
        name="angle_weights",
    )(shifts.reshape(1, -1), angle_map)


def products(na, shots, slot_ref, mw_ref, fwd, rev, obuf, rhs):
    slot = slot_ref[...]
    sub = lax.broadcasted_iota(jnp.int32, (GROUP, LANES), 0)
    steps = 16 // MB

    def fill(rho, mb, buf):
        extra = []
        for m in range(mb * MB, (mb + 1) * MB):
            tot = None
            for s in range(shots):
                t = rev[s, pl.ds(ROWS - 1 - 8 * m - rho, 1), :] * fwd[s, pl.ds(LANES + 8 * m + rho, 1), :]
                tot = t if tot is None else tot + t
            extra.append(jnp.broadcast_to(tot, (GROUP, LANES)))
        for nb in range(16 // NB):
            acc = [[None] * NB for _ in range(MB)]
            for s in range(shots):
                a = {}
                c = {}
                for i in range(MB):
                    for j in range(NB):
                        m, n = mb * MB + i, nb * NB + j
                        if n - m not in a:
                            a[n - m] = rev[s, pl.ds(LANES - 1 - rho + 8 * (n - m), GROUP), :]
                        if n + m not in c:
                            c[n + m] = fwd[s, pl.ds(rho + 8 * (n + m), GROUP), :]
                        t = a[n - m] * c[n + m]
                        acc[i][j] = t if acc[i][j] is None else acc[i][j] + t
            for j in range(0, NB, 2):
                n = nb * NB + j
                masks = [sub == slot - 8 * (n + k) for k in range(2)]
                for i in range(MB):
                    high, low = split(jnp.concatenate([jnp.where(masks[k], extra[i], acc[i][j + k]) for k in range(2)], 0))
                    rhs[buf, 8 * n : 8 * n + 16, i * LANES : (i + 1) * LANES] = high
                    rhs[buf, LANES + 8 * n : LANES + 8 * n + 16, i * LANES : (i + 1) * LANES] = low

    def contract(rho, mb, buf):
        res = jnp.dot(mw_ref[0], rhs[buf], preferred_element_type=jnp.float32)
        res += jnp.dot(mw_ref[1], rhs[buf], preferred_element_type=jnp.float32)
        for i in range(MB):
            obuf[pl.ds(8 * (mb * MB + i) + rho, na, stride=PITCH), :] = res[:, i * LANES : (i + 1) * LANES]

    def turn(rhos):
        items = [(rho, mb) for rho in rhos for mb in range(steps)]
        for i, (rho, mb) in enumerate(items):
            fill(rho, mb, i % 2)
            if i:
                contract(*items[i - 1], (i - 1) % 2)
        contract(*items[-1], (len(items) - 1) % 2)

    if shots <= 4:
        turn(range(GROUP))
    else:

        @pl.loop(0, GROUP)
        def _(rho):
            turn([rho])


def image_body(blocks, shots, *refs):
    given, out_ref = refs[: 5 + shots], refs[5 + shots]
    slot_ref, mw_ref, speed, above, below, held, ext, fwd, rev, obuf, stage, in_sems, out_sems = refs[6 + shots :]
    na, depth, _ = out_ref.shape
    kept = [slot_ref, mw_ref, speed, above, below] + [held.at[s] for s in range(shots)]
    fetches = [pltpu.make_async_copy(x, y, in_sems.at[i]) for i, (x, y) in enumerate(zip(given, kept))]
    for fetch in fetches:
        fetch.start()
    for fetch in fetches:
        fetch.wait()

    zero = jnp.zeros((GROUP, LANES), jnp.float32)
    low = depth - GROUP
    for s in range(shots):
        for f in range(2):
            rim = slice(f * RIM, (f + 1) * RIM)
            for t in range(blocks + 1):
                at = slice(t * LANES, (t + 1) * LANES)
                ext[s, f, t, 0:GROUP, :] = zero
                ext[s, f, t, GROUP : 2 * GROUP, :] = zero
                ext[s, f, t, 2 * GROUP : 3 * GROUP, :] = zero
                ext[s, f, t, 3 * GROUP : 4 * GROUP, :] = zero
                ext[s, f, t, GROUP - RIM : GROUP, :] = above[s, rim, at]
                ext[s, f, t, 3 * GROUP : 3 * GROUP + RIM, :] = below[s, rim, at]
                top, bottom = None, None
                for k in range(1, RIM + 1):
                    u = coeffs[k] * ext[s, f, t, GROUP - k : 2 * GROUP - k, :]
                    v = coeffs[k] * ext[s, f, t, 2 * GROUP + k : 3 * GROUP + k, :]
                    top, bottom = (u, v) if top is None else (top + u, bottom + v)
                held[s, f, 0:GROUP, at] += speed[f, 0:GROUP, at] * top
                held[s, f, low:depth, at] += speed[f, GROUP:, at] * bottom

    def gathered(s, f, b):
        tiles = []
        for q in range(blocks):
            t = q + b if f else blocks - 1 - q + b
            tiles.append(held[s, f, :, t * LANES : (t + 1) * LANES])
        if blocks * depth < LANES:
            tiles.append(jnp.zeros((LANES - blocks * depth, LANES), jnp.float32))
        return jnp.concatenate(tiles, 0)

    for s in range(shots):
        for b in range(2):
            fwd[s, b * LANES : (b + 1) * LANES, :] = gathered(s, 1, b).T
            rev[s, b * LANES : (b + 1) * LANES, :] = gathered(s, 0, b).T

    pl.run_scoped(
        functools.partial(products, na, shots, slot_ref, mw_ref, fwd, rev, obuf),
        pltpu.VMEM((2, ROWS, LANES * MB), jnp.bfloat16),
    )

    def leave(i):
        at = pl.ds(i * APART, APART)
        return pltpu.make_async_copy(stage.at[at], out_ref.at[at], out_sems.at[i])

    @pl.loop(0, na // (2 * APART))
    def _(i):
        for part in range(2):
            for a in range(APART):
                angle = (2 * i + part) * APART + a
                tile = obuf[pl.ds(angle * PITCH, LANES), :].T
                for q in range(blocks):
                    stage[angle, :, q * LANES : (q + 1) * LANES] = tile[q * depth : (q + 1) * depth, :]
            leave(2 * i + part).start()

    @pl.loop(0, na // APART)
    def _(i):
        leave(i).wait()


def angle_image(wins, above, below, speed, mw, slot, depth):
    shots = len(wins)
    full = wins[0].shape[2]
    width = full - 2 * MAXLAG
    na = mw.shape[1]
    anywhere = pl.BlockSpec(memory_space=pl.ANY)
    like = lambda x: pltpu.VMEM(x.shape, x.dtype)
    return pl.pallas_call(
        functools.partial(image_body, width // LANES, shots),
        out_shape=jax.ShapeDtypeStruct((na, depth, width), jnp.float32),
        in_specs=[anywhere] * (5 + shots),
        out_specs=pl.BlockSpec(memory_space=pltpu.HBM),
        scratch_shapes=[
            like(slot),
            like(mw),
            like(speed),
            like(above),
            like(below),
            pltpu.VMEM((shots, *wins[0].shape), jnp.float32),
            pltpu.VMEM((shots, 2, full // LANES, 4 * GROUP, LANES), jnp.float32),
            pltpu.VMEM((shots, ROWS, LANES), jnp.float32),
            pltpu.VMEM((shots, ROWS, LANES), jnp.float32),
            pltpu.VMEM((na * PITCH, LANES), jnp.float32),
            pltpu.VMEM((na, depth, width), jnp.float32),
            pltpu.SemaphoreType.DMA((5 + shots,)),
            pltpu.SemaphoreType.DMA((na // APART,)),
        ],
        compiler_params=pltpu.CompilerParams(vmem_limit_bytes=60 << 20),
        name="angle_image",
    )(slot, mw, speed, above, below, *wins)


def body(src_now, src_prev, rcv_now, rcv_prev, courant, shot_cell, wavelet, shifts, angle_map):
    depth = src_now.shape[1]
    count = lax.axis_size("offset")
    slabs = lax.axis_size("space")

    def exchanged(parts):
        out = [parts[0]]
        for d in range(1, count):
            out.append(lax.ppermute(parts[d], "offset", [(i, i ^ d) for i in range(count)]))
        return out

    speed, rims, wins = stepped_windows(count, shot_cell, wavelet, (src_now, src_prev, rcv_now, rcv_prev, courant))
    rims = exchanged(rims)
    wins = exchanged(wins)
    up, down = rims_by_side(rims)
    below = lax.ppermute(up, "space", [(i + 1, i) for i in range(slabs - 1)])
    above = lax.ppermute(down, "space", [(i, i + 1) for i in range(slabs - 1)])
    mw, slot = angle_weights(shifts, angle_map)
    return angle_image(wins, above, below, speed, mw, slot, depth)


def solution(mesh):
    placed = (
        P("offset", ("groups", "space"), None),
        P("offset", ("groups", "space"), None),
        P("offset", ("groups", "space"), None),
        P("offset", ("groups", "space"), None),
        P(("groups", "space"), None),
        P("groups"),
        P("groups"),
        P(),
        P(),
    )
    step = jax.shard_map(
        body,
        mesh=mesh,
        in_specs=placed,
        out_specs=P(None, ("groups", "space"), "offset"),
        check_vma=False,
    )

    def run(*args):
        with jax.sharding.use_abstract_mesh(mesh.abstract_mesh):
            return step(*args)

    return run
```

```python
import functools

import jax
import jax.numpy as jnp
from jax import lax
from jax.experimental import pallas as pl
from jax.experimental.pallas import tpu as pltpu
from jax.sharding import PartitionSpec as P

MAXLAG = 64
LANES = 128
ROWS = 2 * LANES
GROUP = 8
RIM = 4
PITCH = LANES + 1
MB = 4
NB = 4
APART = 16


coeffs = (-205.0 / 72.0, 8.0 / 5.0, -1.0 / 5.0, 8.0 / 315.0, -1.0 / 560.0)


def split(x):
    high = x.astype(jnp.bfloat16)
    low = (x - high.astype(jnp.float32)).astype(jnp.bfloat16)
    return high, low


def lateral(tiles, lane):
    zero = jnp.zeros_like(tiles[0])
    total = [None] * len(tiles)
    for k in range(1, RIM + 1):
        up = [pltpu.roll(v, k, 1) for v in tiles]
        down = [pltpu.roll(v, LANES - k, 1) for v in tiles]
        for t in range(len(tiles)):
            left = jnp.where(lane < k, up[t - 1] if t else zero, up[t])
            right = jnp.where(lane >= LANES - k, down[t + 1] if t + 1 < len(tiles) else zero, down[t])
            term = coeffs[k] * (left + right)
            total[t] = term if total[t] is None else total[t] + term
    return total


def step_body(width, cell_ref, amp_ref, src_now, src_prev, rcv_now, rcv_prev, courant, speed_ref, *refs):
    count = (len(refs) - 4) // 3
    tops, bottoms, wins = refs[:count], refs[count : 2 * count], refs[2 * count : 3 * count]
    rows_ref, padded, padded_rim, padded_speed = refs[3 * count :]
    depth, nx = src_now.shape[1:]
    blocks = nx // LANES
    me = lax.axis_index("offset")
    cell = cell_ref[me] - lax.axis_index("space") * depth * nx
    amp = amp_ref[me]
    lane = lax.broadcasted_iota(jnp.int32, (GROUP, LANES), 1)
    flat = lax.broadcasted_iota(jnp.int32, (GROUP, LANES), 0) * nx + lane
    source = lax.broadcasted_iota(jnp.int32, (LANES, LANES), 0)
    target = lax.broadcasted_iota(jnp.int32, (LANES, LANES), 1)
    mirror = (lax.rem(source + target + 1, LANES) == MAXLAG).astype(jnp.float32)
    half = lane < MAXLAG
    zero = jnp.zeros((GROUP, LANES), jnp.float32)

    def place(ref, f, row, out):
        if f == 0:
            turned = jnp.dot(
                jnp.concatenate(out[::-1], 0), mirror, precision=lax.Precision.HIGHEST, preferred_element_type=jnp.float32
            )
            out = [turned[t * GROUP : (t + 1) * GROUP, :] for t in range(blocks)]
        else:
            out = [pltpu.roll(v, MAXLAG, 1) for v in out]
        out = [zero] + out + [zero]
        for t in range(blocks + 1):
            ref[f, row : row + GROUP, t * LANES : (t + 1) * LANES] = jnp.where(half, out[t], out[t + 1])

    cuts = [slice(t * LANES, (t + 1) * LANES) for t in range(blocks)]
    nows, prevs = (src_now, rcv_now), (src_prev, rcv_prev)
    for f in range(2):
        now = nows[f]
        place(padded_rim, f, 0, [jnp.concatenate([now[0, :RIM, at], now[0, depth - RIM :, at]], 0) for at in cuts])
        for b, z in enumerate((0, depth - GROUP)):
            place(padded_speed, f, b * GROUP, [courant[z : z + GROUP, at] for at in cuts])
        for t in range(blocks):
            rows_ref[f, t, 0:GROUP, :] = zero
            rows_ref[f, t, GROUP : GROUP + depth, :] = now[0, :, cuts[t]]
            rows_ref[f, t, GROUP + depth : 2 * GROUP + depth, :] = zero
        for z in range(0, depth, GROUP):
            at = z + GROUP
            tiles = [rows_ref[f, t, at : at + GROUP, :] for t in range(blocks)]
            across = lateral(tiles, lane)
            out = []
            for t in range(blocks):
                total = (2.0 * coeffs[0]) * tiles[t] + across[t]
                for k in range(1, RIM + 1):
                    total = total + coeffs[k] * (rows_ref[f, t, at - k : at - k + GROUP, :] + rows_ref[f, t, at + k : at + k + GROUP, :])
                value = 2.0 * tiles[t] - prevs[f][0, z : z + GROUP, cuts[t]] + courant[z : z + GROUP, cuts[t]] * total
                if f == 0:
                    value = value + jnp.where(flat == cell - (z * nx + t * LANES), amp, 0.0)
                out.append(value)
            place(padded, f, z, out)
    for d in range(count):
        other = lax.bitwise_xor(me, d)
        for f, first in enumerate((count - 1 - other, other)):
            at = pl.ds(pl.multiple_of(first * width, LANES), width + 2 * MAXLAG)
            tops[d][f] = padded_rim[f, :RIM, at]
            bottoms[d][f] = padded_rim[f, RIM:, at]
            wins[d][f] = padded[f, :, at]
            if d == 0:
                speed_ref[f] = padded_speed[f, :, at]


def stepped_windows(count, cell, amp, fields):
    depth, nx = fields[0].shape[1:]
    width = nx // count
    shape = lambda rows: jax.ShapeDtypeStruct((2, rows, width + 2 * MAXLAG), jnp.float32)
    smem = pl.BlockSpec(memory_space=pltpu.SMEM)
    vmem = pl.BlockSpec(memory_space=pltpu.VMEM)
    speed, *rest = pl.pallas_call(
        functools.partial(step_body, width),
        in_specs=[smem, smem] + [vmem] * len(fields),
        out_specs=[vmem] * (1 + 3 * count),
        out_shape=[shape(2 * GROUP)] + [shape(RIM)] * (2 * count) + [shape(depth)] * count,
        scratch_shapes=[
            pltpu.VMEM((2, nx // LANES, depth + 2 * GROUP, LANES), jnp.float32),
            pltpu.VMEM((2, depth, nx + 2 * MAXLAG), jnp.float32),
            pltpu.VMEM((2, GROUP, nx + 2 * MAXLAG), jnp.float32),
            pltpu.VMEM((2, 2 * GROUP, nx + 2 * MAXLAG), jnp.float32),
        ],
        compiler_params=pltpu.CompilerParams(vmem_limit_bytes=60 << 20),
        name="step",
    )(cell, amp, *fields)
    return speed, rest[:count], rest[count : 2 * count], rest[2 * count :]


def weight_body(shift_ref, map_ref, mw_ref, slot_ref):
    lag = lax.broadcasted_iota(jnp.int32, (ROWS, LANES), 0) - MAXLAG
    hot = jnp.where(lag == shift_ref[...], 1.0, 0.0)
    full = lax.dot_general(
        map_ref[...], hot, (((1,), (1,)), ((), ())), precision=lax.Precision.HIGHEST, preferred_element_type=jnp.float32
    )
    na = full.shape[0]
    used = jnp.max(hot[:LANES, :], axis=1, keepdims=True)
    k = lax.broadcasted_iota(jnp.int32, (LANES, 1), 0).astype(jnp.float32)
    slot = jnp.min(jnp.where(used > 0.0, float(ROWS), k), axis=0, keepdims=True).astype(jnp.int32)
    column = lax.broadcasted_iota(jnp.int32, (na, LANES), 1)
    w = jnp.where(column == slot, full[:, LANES : LANES + 1], full[:, :LANES])
    high, low = split(w)
    mw_ref[0, :, :LANES] = high
    mw_ref[0, :, LANES:] = high
    mw_ref[1, :, :LANES] = low
    mw_ref[1, :, LANES:] = jnp.zeros_like(low)
    slot_ref[...] = jnp.broadcast_to(slot, slot_ref.shape)


def angle_weights(shifts, angle_map):
    na = angle_map.shape[0]
    return pl.pallas_call(
        weight_body,
        out_shape=[jax.ShapeDtypeStruct((2, na, ROWS), jnp.bfloat16), jax.ShapeDtypeStruct((GROUP, LANES), jnp.int32)],
        compiler_params=pltpu.CompilerParams(vmem_limit_bytes=60 << 20),
        name="angle_weights",
    )(shifts.reshape(1, -1), angle_map)


def products(na, shots, slot_ref, mw_ref, fwd, rev, obuf, rhs):
    slot = slot_ref[...]
    sub = lax.broadcasted_iota(jnp.int32, (GROUP, LANES), 0)
    steps = 16 // MB

    def fill(rho, mb, buf):
        extra = []
        for m in range(mb * MB, (mb + 1) * MB):
            tot = None
            for s in range(shots):
                t = rev[s, pl.ds(ROWS - 1 - 8 * m - rho, 1), :] * fwd[s, pl.ds(LANES + 8 * m + rho, 1), :]
                tot = t if tot is None else tot + t
            extra.append(jnp.broadcast_to(tot, (GROUP, LANES)))
        for nb in range(16 // NB):
            acc = [[None] * NB for _ in range(MB)]
            for s in range(shots):
                a = {}
                c = {}
                for i in range(MB):
                    for j in range(NB):
                        m, n = mb * MB + i, nb * NB + j
                        if n - m not in a:
                            a[n - m] = rev[s, pl.ds(LANES - 1 - rho + 8 * (n - m), GROUP), :]
                        if n + m not in c:
                            c[n + m] = fwd[s, pl.ds(rho + 8 * (n + m), GROUP), :]
                        t = a[n - m] * c[n + m]
                        acc[i][j] = t if acc[i][j] is None else acc[i][j] + t
            for j in range(0, NB, 2):
                n = nb * NB + j
                masks = [sub == slot - 8 * (n + k) for k in range(2)]
                for i in range(MB):
                    high, low = split(jnp.concatenate([jnp.where(masks[k], extra[i], acc[i][j + k]) for k in range(2)], 0))
                    rhs[buf, 8 * n : 8 * n + 16, i * LANES : (i + 1) * LANES] = high
                    rhs[buf, LANES + 8 * n : LANES + 8 * n + 16, i * LANES : (i + 1) * LANES] = low

    def contract(rho, mb, buf):
        res = jnp.dot(mw_ref[0], rhs[buf], preferred_element_type=jnp.float32)
        res += jnp.dot(mw_ref[1], rhs[buf], preferred_element_type=jnp.float32)
        for i in range(MB):
            obuf[pl.ds(8 * (mb * MB + i) + rho, na, stride=PITCH), :] = res[:, i * LANES : (i + 1) * LANES]

    def turn(rhos):
        items = [(rho, mb) for rho in rhos for mb in range(steps)]
        for i, (rho, mb) in enumerate(items):
            fill(rho, mb, i % 2)
            if i:
                contract(*items[i - 1], (i - 1) % 2)
        contract(*items[-1], (len(items) - 1) % 2)

    if shots <= 4:
        turn(range(GROUP))
    else:

        @pl.loop(0, GROUP)
        def _(rho):
            turn([rho])


def image_body(blocks, shots, *refs):
    given, out_ref = refs[: 3 + 3 * shots], refs[3 + 3 * shots]
    slot_ref, mw_ref, speed, above, below, held, ext, fwd, rev, obuf, stage, in_sems, out_sems = refs[4 + 3 * shots :]
    na, depth, _ = out_ref.shape
    kept = [slot_ref, mw_ref, speed] + [x.at[s] for x in (above, below, held) for s in range(shots)]
    fetches = [pltpu.make_async_copy(x, y, in_sems.at[i]) for i, (x, y) in enumerate(zip(given, kept))]
    for fetch in fetches:
        fetch.start()
    for fetch in fetches:
        fetch.wait()

    zero = jnp.zeros((GROUP, LANES), jnp.float32)
    low = depth - GROUP
    for s in range(shots):
        for f in range(2):
            for t in range(blocks + 1):
                at = slice(t * LANES, (t + 1) * LANES)
                ext[s, f, t, 0:GROUP, :] = zero
                ext[s, f, t, GROUP : 2 * GROUP, :] = zero
                ext[s, f, t, 2 * GROUP : 3 * GROUP, :] = zero
                ext[s, f, t, 3 * GROUP : 4 * GROUP, :] = zero
                ext[s, f, t, GROUP - RIM : GROUP, :] = above[s, f, :, at]
                ext[s, f, t, 3 * GROUP : 3 * GROUP + RIM, :] = below[s, f, :, at]
                top, bottom = None, None
                for k in range(1, RIM + 1):
                    u = coeffs[k] * ext[s, f, t, GROUP - k : 2 * GROUP - k, :]
                    v = coeffs[k] * ext[s, f, t, 2 * GROUP + k : 3 * GROUP + k, :]
                    top, bottom = (u, v) if top is None else (top + u, bottom + v)
                held[s, f, 0:GROUP, at] += speed[f, 0:GROUP, at] * top
                held[s, f, low:depth, at] += speed[f, GROUP:, at] * bottom

    def gathered(s, f, b):
        tiles = []
        for q in range(blocks):
            t = q + b if f else blocks - 1 - q + b
            tiles.append(held[s, f, :, t * LANES : (t + 1) * LANES])
        if blocks * depth < LANES:
            tiles.append(jnp.zeros((LANES - blocks * depth, LANES), jnp.float32))
        return jnp.concatenate(tiles, 0)

    for s in range(shots):
        for b in range(2):
            fwd[s, b * LANES : (b + 1) * LANES, :] = gathered(s, 1, b).T
            rev[s, b * LANES : (b + 1) * LANES, :] = gathered(s, 0, b).T

    pl.run_scoped(
        functools.partial(products, na, shots, slot_ref, mw_ref, fwd, rev, obuf),
        pltpu.VMEM((2, ROWS, LANES * MB), jnp.bfloat16),
    )

    def leave(i):
        at = pl.ds(i * APART, APART)
        return pltpu.make_async_copy(stage.at[at], out_ref.at[at], out_sems.at[i])

    @pl.loop(0, na // (2 * APART))
    def _(i):
        for part in range(2):
            for a in range(APART):
                angle = (2 * i + part) * APART + a
                tile = obuf[pl.ds(angle * PITCH, LANES), :].T
                for q in range(blocks):
                    stage[angle, :, q * LANES : (q + 1) * LANES] = tile[q * depth : (q + 1) * depth, :]
            leave(2 * i + part).start()

    @pl.loop(0, na // APART)
    def _(i):
        leave(i).wait()


def angle_image(wins, above, below, speed, mw, slot, depth):
    shots = len(wins)
    full = wins[0].shape[2]
    width = full - 2 * MAXLAG
    na = mw.shape[1]
    anywhere = pl.BlockSpec(memory_space=pl.ANY)
    like = lambda x: pltpu.VMEM(x.shape, x.dtype)
    return pl.pallas_call(
        functools.partial(image_body, width // LANES, shots),
        out_shape=jax.ShapeDtypeStruct((na, depth, width), jnp.float32),
        in_specs=[anywhere] * (3 + 3 * shots),
        out_specs=pl.BlockSpec(memory_space=pltpu.HBM),
        scratch_shapes=[
            like(slot),
            like(mw),
            like(speed),
            pltpu.VMEM((shots, *above[0].shape), jnp.float32),
            pltpu.VMEM((shots, *below[0].shape), jnp.float32),
            pltpu.VMEM((shots, *wins[0].shape), jnp.float32),
            pltpu.VMEM((shots, 2, full // LANES, 4 * GROUP, LANES), jnp.float32),
            pltpu.VMEM((shots, ROWS, LANES), jnp.float32),
            pltpu.VMEM((shots, ROWS, LANES), jnp.float32),
            pltpu.VMEM((na * PITCH, LANES), jnp.float32),
            pltpu.VMEM((na, depth, width), jnp.float32),
            pltpu.SemaphoreType.DMA((3 + 3 * shots,)),
            pltpu.SemaphoreType.DMA((na // APART,)),
        ],
        compiler_params=pltpu.CompilerParams(vmem_limit_bytes=60 << 20),
        name="angle_image",
    )(slot, mw, speed, *above, *below, *wins)


def body(src_now, src_prev, rcv_now, rcv_prev, courant, shot_cell, wavelet, shifts, angle_map):
    depth = src_now.shape[1]
    count = lax.axis_size("offset")
    slabs = lax.axis_size("space")

    def exchanged(parts):
        out = [parts[0]]
        for d in range(1, count):
            out.append(lax.ppermute(parts[d], "offset", [(i, i ^ d) for i in range(count)]))
        return out

    def from_slab(parts, side):
        out = []
        for d in range(count):
            pairs = [
                (i * slabs + z, (i ^ d) * slabs + z + side)
                for z in range(slabs)
                if 0 <= z + side < slabs
                for i in range(count)
            ]
            out.append(lax.ppermute(parts[d], ("offset", "space"), pairs))
        return out

    speed, tops, bottoms, wins = stepped_windows(
        count, shot_cell, wavelet, (src_now, src_prev, rcv_now, rcv_prev, courant)
    )
    wins = exchanged(wins)
    below = from_slab(tops, -1)
    above = from_slab(bottoms, 1)
    mw, slot = angle_weights(shifts, angle_map)
    return angle_image(wins, above, below, speed, mw, slot, depth)


def solution(mesh):
    placed = (
        P("offset", ("groups", "space"), None),
        P("offset", ("groups", "space"), None),
        P("offset", ("groups", "space"), None),
        P("offset", ("groups", "space"), None),
        P(("groups", "space"), None),
        P("groups"),
        P("groups"),
        P(),
        P(),
    )
    step = jax.shard_map(
        body,
        mesh=mesh,
        in_specs=placed,
        out_specs=P(None, ("groups", "space"), "offset"),
        check_vma=False,
    )

    def run(*args):
        with jax.sharding.use_abstract_mesh(mesh.abstract_mesh):
            return step(*args)

    return run
```

```python
import functools

import jax
import jax.numpy as jnp
from jax import lax
from jax.experimental import pallas as pl
from jax.experimental.pallas import tpu as pltpu
from jax.sharding import PartitionSpec as P

MAXLAG = 64
LANES = 128
ROWS = 2 * LANES
GROUP = 8
RIM = 4
PITCH = LANES + 1
MB = 4
NB = 4
APART = 16


coeffs = (-205.0 / 72.0, 8.0 / 5.0, -1.0 / 5.0, 8.0 / 315.0, -1.0 / 560.0)


def split(x):
    high = x.astype(jnp.bfloat16)
    low = (x - high.astype(jnp.float32)).astype(jnp.bfloat16)
    return high, low


def lateral(tiles, lane):
    zero = jnp.zeros_like(tiles[0])
    total = [None] * len(tiles)
    for k in range(1, RIM + 1):
        up = [pltpu.roll(v, k, 1) for v in tiles]
        down = [pltpu.roll(v, LANES - k, 1) for v in tiles]
        for t in range(len(tiles)):
            left = jnp.where(lane < k, up[t - 1] if t else zero, up[t])
            right = jnp.where(lane >= LANES - k, down[t + 1] if t + 1 < len(tiles) else zero, down[t])
            term = coeffs[k] * (left + right)
            total[t] = term if total[t] is None else total[t] + term
    return total


def place(ref, f, row, out):
    blocks = len(out)
    if f == 0:
        source = lax.broadcasted_iota(jnp.int32, (LANES, LANES), 0)
        target = lax.broadcasted_iota(jnp.int32, (LANES, LANES), 1)
        mirror = (lax.rem(source + target + 1, LANES) == MAXLAG).astype(jnp.float32)
        turned = jnp.dot(
            jnp.concatenate(out[::-1], 0), mirror, precision=lax.Precision.HIGHEST, preferred_element_type=jnp.float32
        )
        out = [turned[t * GROUP : (t + 1) * GROUP, :] for t in range(blocks)]
    else:
        out = [pltpu.roll(v, MAXLAG, 1) for v in out]
    half = lax.broadcasted_iota(jnp.int32, (GROUP, LANES), 1) < MAXLAG
    zero = jnp.zeros((GROUP, LANES), jnp.float32)
    out = [zero] + out + [zero]
    for t in range(blocks + 1):
        ref[f, row : row + GROUP, t * LANES : (t + 1) * LANES] = jnp.where(half, out[t], out[t + 1])


def window_at(me, d, f, count, width):
    other = lax.bitwise_xor(me, d)
    first = other if f else count - 1 - other
    return pl.ds(pl.multiple_of(first * width, LANES), width + 2 * MAXLAG)


def step_body(width, cell_ref, amp_ref, src_now, src_prev, rcv_now, rcv_prev, courant, up_ref, down_ref, speed_ref, *refs):
    wins = refs[:-3]
    count = len(wins)
    rows_ref, padded, padded_speed = refs[-3:]
    depth, nx = src_now.shape[1:]
    blocks = nx // LANES
    me = lax.axis_index("offset")
    cell = cell_ref[me] - lax.axis_index("space") * depth * nx
    amp = amp_ref[me]
    lane = lax.broadcasted_iota(jnp.int32, (GROUP, LANES), 1)
    flat = lax.broadcasted_iota(jnp.int32, (GROUP, LANES), 0) * nx + lane
    zero = jnp.zeros((GROUP, LANES), jnp.float32)
    cuts = [slice(t * LANES, (t + 1) * LANES) for t in range(blocks)]
    nows, prevs = (src_now, rcv_now), (src_prev, rcv_prev)
    for f in range(2):
        now = nows[f]
        up_ref[f * RIM : (f + 1) * RIM, :] = now[0, :RIM, :]
        down_ref[f * RIM : (f + 1) * RIM, :] = now[0, depth - RIM :, :]
        for b, z in enumerate((0, depth - GROUP)):
            place(padded_speed, f, b * GROUP, [courant[z : z + GROUP, at] for at in cuts])
        for t in range(blocks):
            rows_ref[f, t, 0:GROUP, :] = zero
            rows_ref[f, t, GROUP : GROUP + depth, :] = now[0, :, cuts[t]]
            rows_ref[f, t, GROUP + depth : 2 * GROUP + depth, :] = zero
        for z in range(0, depth, GROUP):
            at = z + GROUP
            tiles = [rows_ref[f, t, at : at + GROUP, :] for t in range(blocks)]
            across = lateral(tiles, lane)
            out = []
            for t in range(blocks):
                total = (2.0 * coeffs[0]) * tiles[t] + across[t]
                for k in range(1, RIM + 1):
                    total = total + coeffs[k] * (rows_ref[f, t, at - k : at - k + GROUP, :] + rows_ref[f, t, at + k : at + k + GROUP, :])
                value = 2.0 * tiles[t] - prevs[f][0, z : z + GROUP, cuts[t]] + courant[z : z + GROUP, cuts[t]] * total
                if f == 0:
                    value = value + jnp.where(flat == cell - (z * nx + t * LANES), amp, 0.0)
                out.append(value)
            place(padded, f, z, out)
    for f in range(2):
        speed_ref[f] = padded_speed[f, :, window_at(me, 0, f, count, width)]
        for d in range(count):
            wins[d][f] = padded[f, :, window_at(me, d, f, count, width)]


def rim_body(width, above, below, *refs):
    outs, padded = refs[:-1], refs[-1]
    count = len(outs)
    me = lax.axis_index("offset")
    for f in range(2):
        rim = slice(f * RIM, (f + 1) * RIM)
        cuts = [slice(t * LANES, (t + 1) * LANES) for t in range(above.shape[1] // LANES)]
        place(padded, f, 0, [jnp.concatenate([above[rim, at], below[rim, at]], 0) for at in cuts])
        for d in range(count):
            outs[d][f] = padded[f, :, window_at(me, d, f, count, width)]


def rim_windows(count, above, below):
    nx = above.shape[1]
    width = nx // count
    return pl.pallas_call(
        functools.partial(rim_body, width),
        in_specs=[pl.BlockSpec(memory_space=pltpu.VMEM)] * 2,
        out_specs=[pl.BlockSpec(memory_space=pltpu.VMEM)] * count,
        out_shape=[jax.ShapeDtypeStruct((2, GROUP, width + 2 * MAXLAG), jnp.float32)] * count,
        scratch_shapes=[pltpu.VMEM((2, GROUP, nx + 2 * MAXLAG), jnp.float32)],
        compiler_params=pltpu.CompilerParams(vmem_limit_bytes=8 << 20),
        name="rim_windows",
    )(above, below)


def stepped_windows(count, cell, amp, fields):
    depth, nx = fields[0].shape[1:]
    width = nx // count
    shape = lambda rows: jax.ShapeDtypeStruct((2, rows, width + 2 * MAXLAG), jnp.float32)
    smem = pl.BlockSpec(memory_space=pltpu.SMEM)
    vmem = pl.BlockSpec(memory_space=pltpu.VMEM)
    rim = jax.ShapeDtypeStruct((2 * RIM, nx), jnp.float32)
    up, down, speed, *wins = pl.pallas_call(
        functools.partial(step_body, width),
        in_specs=[smem, smem] + [vmem] * len(fields),
        out_specs=[vmem] * (3 + count),
        out_shape=[rim, rim, shape(2 * GROUP)] + [shape(depth)] * count,
        scratch_shapes=[
            pltpu.VMEM((2, nx // LANES, depth + 2 * GROUP, LANES), jnp.float32),
            pltpu.VMEM((2, depth, nx + 2 * MAXLAG), jnp.float32),
            pltpu.VMEM((2, 2 * GROUP, nx + 2 * MAXLAG), jnp.float32),
        ],
        compiler_params=pltpu.CompilerParams(vmem_limit_bytes=60 << 20),
        name="step",
    )(cell, amp, *fields)
    return up, down, speed, wins


def weight_body(shift_ref, map_ref, mw_ref, slot_ref):
    lag = lax.broadcasted_iota(jnp.int32, (ROWS, LANES), 0) - MAXLAG
    hot = jnp.where(lag == shift_ref[...], 1.0, 0.0)
    full = lax.dot_general(
        map_ref[...], hot, (((1,), (1,)), ((), ())), precision=lax.Precision.HIGHEST, preferred_element_type=jnp.float32
    )
    na = full.shape[0]
    used = jnp.max(hot[:LANES, :], axis=1, keepdims=True)
    k = lax.broadcasted_iota(jnp.int32, (LANES, 1), 0).astype(jnp.float32)
    slot = jnp.min(jnp.where(used > 0.0, float(ROWS), k), axis=0, keepdims=True).astype(jnp.int32)
    column = lax.broadcasted_iota(jnp.int32, (na, LANES), 1)
    w = jnp.where(column == slot, full[:, LANES : LANES + 1], full[:, :LANES])
    high, low = split(w)
    mw_ref[0, :, :LANES] = high
    mw_ref[0, :, LANES:] = high
    mw_ref[1, :, :LANES] = low
    mw_ref[1, :, LANES:] = jnp.zeros_like(low)
    slot_ref[...] = jnp.broadcast_to(slot, slot_ref.shape)


def angle_weights(shifts, angle_map):
    na = angle_map.shape[0]
    return pl.pallas_call(
        weight_body,
        out_shape=[jax.ShapeDtypeStruct((2, na, ROWS), jnp.bfloat16), jax.ShapeDtypeStruct((GROUP, LANES), jnp.int32)],
        compiler_params=pltpu.CompilerParams(vmem_limit_bytes=60 << 20),
        name="angle_weights",
    )(shifts.reshape(1, -1), angle_map)


def products(na, shots, slot_ref, mw_ref, fwd, rev, obuf, rhs):
    slot = slot_ref[...]
    sub = lax.broadcasted_iota(jnp.int32, (GROUP, LANES), 0)
    steps = 16 // MB

    def fill(rho, mb, buf):
        extra = []
        for m in range(mb * MB, (mb + 1) * MB):
            tot = None
            for s in range(shots):
                t = rev[s, pl.ds(ROWS - 1 - 8 * m - rho, 1), :] * fwd[s, pl.ds(LANES + 8 * m + rho, 1), :]
                tot = t if tot is None else tot + t
            extra.append(jnp.broadcast_to(tot, (GROUP, LANES)))
        for nb in range(16 // NB):
            acc = [[None] * NB for _ in range(MB)]
            for s in range(shots):
                a = {}
                c = {}
                for i in range(MB):
                    for j in range(NB):
                        m, n = mb * MB + i, nb * NB + j
                        if n - m not in a:
                            a[n - m] = rev[s, pl.ds(LANES - 1 - rho + 8 * (n - m), GROUP), :]
                        if n + m not in c:
                            c[n + m] = fwd[s, pl.ds(rho + 8 * (n + m), GROUP), :]
                        t = a[n - m] * c[n + m]
                        acc[i][j] = t if acc[i][j] is None else acc[i][j] + t
            for j in range(0, NB, 2):
                n = nb * NB + j
                masks = [sub == slot - 8 * (n + k) for k in range(2)]
                for i in range(MB):
                    high, low = split(jnp.concatenate([jnp.where(masks[k], extra[i], acc[i][j + k]) for k in range(2)], 0))
                    rhs[buf, 8 * n : 8 * n + 16, i * LANES : (i + 1) * LANES] = high
                    rhs[buf, LANES + 8 * n : LANES + 8 * n + 16, i * LANES : (i + 1) * LANES] = low

    def contract(rho, mb, buf):
        res = jnp.dot(mw_ref[0], rhs[buf], preferred_element_type=jnp.float32)
        res += jnp.dot(mw_ref[1], rhs[buf], preferred_element_type=jnp.float32)
        for i in range(MB):
            obuf[pl.ds(8 * (mb * MB + i) + rho, na, stride=PITCH), :] = res[:, i * LANES : (i + 1) * LANES]

    def turn(rhos):
        items = [(rho, mb) for rho in rhos for mb in range(steps)]
        for i, (rho, mb) in enumerate(items):
            fill(rho, mb, i % 2)
            if i:
                contract(*items[i - 1], (i - 1) % 2)
        contract(*items[-1], (len(items) - 1) % 2)

    if shots <= 4:
        turn(range(GROUP))
    else:

        @pl.loop(0, GROUP)
        def _(rho):
            turn([rho])


def image_body(blocks, shots, *refs):
    given, out_ref = refs[: 3 + 2 * shots], refs[3 + 2 * shots]
    slot_ref, mw_ref, speed, rims, held, ext, fwd, rev, obuf, stage, in_sems, out_sems = refs[4 + 2 * shots :]
    na, depth, _ = out_ref.shape
    kept = [slot_ref, mw_ref, speed] + [x.at[s] for x in (rims, held) for s in range(shots)]
    fetches = [pltpu.make_async_copy(x, y, in_sems.at[i]) for i, (x, y) in enumerate(zip(given, kept))]
    for fetch in fetches:
        fetch.start()
    for fetch in fetches:
        fetch.wait()

    zero = jnp.zeros((GROUP, LANES), jnp.float32)
    low = depth - GROUP
    for s in range(shots):
        for f in range(2):
            for t in range(blocks + 1):
                at = slice(t * LANES, (t + 1) * LANES)
                ext[s, f, t, 0:GROUP, :] = zero
                ext[s, f, t, GROUP : 2 * GROUP, :] = zero
                ext[s, f, t, 2 * GROUP : 3 * GROUP, :] = zero
                ext[s, f, t, 3 * GROUP : 4 * GROUP, :] = zero
                ext[s, f, t, GROUP - RIM : GROUP, :] = rims[s, f, :RIM, at]
                ext[s, f, t, 3 * GROUP : 3 * GROUP + RIM, :] = rims[s, f, RIM:, at]
                top, bottom = None, None
                for k in range(1, RIM + 1):
                    u = coeffs[k] * ext[s, f, t, GROUP - k : 2 * GROUP - k, :]
                    v = coeffs[k] * ext[s, f, t, 2 * GROUP + k : 3 * GROUP + k, :]
                    top, bottom = (u, v) if top is None else (top + u, bottom + v)
                held[s, f, 0:GROUP, at] += speed[f, 0:GROUP, at] * top
                held[s, f, low:depth, at] += speed[f, GROUP:, at] * bottom

    def gathered(s, f, b):
        tiles = []
        for q in range(blocks):
            t = q + b if f else blocks - 1 - q + b
            tiles.append(held[s, f, :, t * LANES : (t + 1) * LANES])
        if blocks * depth < LANES:
            tiles.append(jnp.zeros((LANES - blocks * depth, LANES), jnp.float32))
        return jnp.concatenate(tiles, 0)

    for s in range(shots):
        for b in range(2):
            fwd[s, b * LANES : (b + 1) * LANES, :] = gathered(s, 1, b).T
            rev[s, b * LANES : (b + 1) * LANES, :] = gathered(s, 0, b).T

    pl.run_scoped(
        functools.partial(products, na, shots, slot_ref, mw_ref, fwd, rev, obuf),
        pltpu.VMEM((2, ROWS, LANES * MB), jnp.bfloat16),
    )

    def leave(i):
        at = pl.ds(i * APART, APART)
        return pltpu.make_async_copy(stage.at[at], out_ref.at[at], out_sems.at[i])

    @pl.loop(0, na // (2 * APART))
    def _(i):
        for part in range(2):
            for a in range(APART):
                angle = (2 * i + part) * APART + a
                tile = obuf[pl.ds(angle * PITCH, LANES), :].T
                for q in range(blocks):
                    stage[angle, :, q * LANES : (q + 1) * LANES] = tile[q * depth : (q + 1) * depth, :]
            leave(2 * i + part).start()

    @pl.loop(0, na // APART)
    def _(i):
        leave(i).wait()


def angle_image(wins, rims, speed, mw, slot, depth):
    shots = len(wins)
    full = wins[0].shape[2]
    width = full - 2 * MAXLAG
    na = mw.shape[1]
    anywhere = pl.BlockSpec(memory_space=pl.ANY)
    like = lambda x: pltpu.VMEM(x.shape, x.dtype)
    return pl.pallas_call(
        functools.partial(image_body, width // LANES, shots),
        out_shape=jax.ShapeDtypeStruct((na, depth, width), jnp.float32),
        in_specs=[anywhere] * (3 + 2 * shots),
        out_specs=pl.BlockSpec(memory_space=pltpu.HBM),
        scratch_shapes=[
            like(slot),
            like(mw),
            like(speed),
            pltpu.VMEM((shots, *rims[0].shape), jnp.float32),
            pltpu.VMEM((shots, *wins[0].shape), jnp.float32),
            pltpu.VMEM((shots, 2, full // LANES, 4 * GROUP, LANES), jnp.float32),
            pltpu.VMEM((shots, ROWS, LANES), jnp.float32),
            pltpu.VMEM((shots, ROWS, LANES), jnp.float32),
            pltpu.VMEM((na * PITCH, LANES), jnp.float32),
            pltpu.VMEM((na, depth, width), jnp.float32),
            pltpu.SemaphoreType.DMA((3 + 2 * shots,)),
            pltpu.SemaphoreType.DMA((na // APART,)),
        ],
        compiler_params=pltpu.CompilerParams(vmem_limit_bytes=60 << 20),
        name="angle_image",
    )(slot, mw, speed, *rims, *wins)


def body(src_now, src_prev, rcv_now, rcv_prev, courant, shot_cell, wavelet, shifts, angle_map):
    depth = src_now.shape[1]
    count = lax.axis_size("offset")
    slabs = lax.axis_size("space")

    def exchanged(parts):
        out = [parts[0]]
        for d in range(1, count):
            out.append(lax.ppermute(parts[d], "offset", [(i, i ^ d) for i in range(count)]))
        return out

    up, down, speed, wins = stepped_windows(count, shot_cell, wavelet, (src_now, src_prev, rcv_now, rcv_prev, courant))
    wins = exchanged(wins)
    below = lax.ppermute(up, "space", [(i + 1, i) for i in range(slabs - 1)])
    above = lax.ppermute(down, "space", [(i, i + 1) for i in range(slabs - 1)])
    mw, slot = angle_weights(shifts, angle_map)
    rims = exchanged(rim_windows(count, above, below))
    return angle_image(wins, rims, speed, mw, slot, depth)


def solution(mesh):
    placed = (
        P("offset", ("groups", "space"), None),
        P("offset", ("groups", "space"), None),
        P("offset", ("groups", "space"), None),
        P("offset", ("groups", "space"), None),
        P(("groups", "space"), None),
        P("groups"),
        P("groups"),
        P(),
        P(),
    )
    step = jax.shard_map(
        body,
        mesh=mesh,
        in_specs=placed,
        out_specs=P(None, ("groups", "space"), "offset"),
        check_vma=False,
    )

    def run(*args):
        with jax.sharding.use_abstract_mesh(mesh.abstract_mesh):
            return step(*args)

    return run
```
